256 devices in a mesh: section: 4 (over y_hi, core), expert: 64 (over y_lo, x, z).
Axes of the slice: x: 4, y: 4 (y_hi: 2, y_lo: 2; y = y_hi * 2 + y_lo), z: 8, core: 2. Of those that a mesh axis runs over, the one named last changes fastest.
Arguments:
- grad_out: bfloat16 [4, 2, 4096, 3584], P('section', None, 'expert'), may hold values from -6 to 6
- gate_probs: bfloat16 [4, 2, 4096, 2], P('section', None, 'expert'), may hold values from 0.049804688 to 1
- routes: int32 [4, 2, 4096, 2], P('section', None, 'expert'), may hold values from 0 to 15, all different within a row; in each aligned block of 64 rows (0 to 63, 64 to 127, ..., all dimensions but the last counted through in order) at most 12 rows name the same one
- saved_preacts: bfloat16 [4, 2, 64, 64, 12, 512], P('section', None, 'expert'), may hold values from -6 to 6
- w_gate_up: bfloat16 [4, 64, 3584, 512], P('section', 'expert'), may hold values from -0.09375 to 0.09375
- w_down: bfloat16 [4, 64, 256, 3584], P('section', 'expert'), may hold values from -0.1875 to 0.1875
Outputs:
- from_above: bfloat16 [4, 4096, 3584], P('section', 'expert')
- from_below: bfloat16 [4, 4096, 3584], P('section', 'expert')
- prob_grad: float32 [4, 2, 4096, 2], P('section', None, 'expert')
- down_grad: bfloat16 [4, 64, 256, 3584], P('section', 'expert')
The draws below stay inside these ranges and needn't reach their ends.
Inputs may be any that keep to these rules, and one draw needn't show every extreme that they name: `routes`: each row names 2 different experts; within the 64 rows of one device for one section and stretch no expert is named by more than 12 rows, a bound that some block reaches.
All inputs are finite; a program needn't handle non-finite values.
Results may differ from the reference program's by a relative error of at most 0.015.
Values may be sent and summed in bfloat16 or wider, within the bound.
No kernel may reach another device: no remote copies, remote signals or barrier semaphores. Data moves between devices by JAX's collectives and lax.ppermute only.
A program may use at most 192 MiB of HBM per device.

```python
import math
import jax
import jax.numpy as jnp
import numpy as np
from jax import lax

D = 3584
FF = 1024
SHARE = 4
TOP = 2
TOK_DEV = 64
SECTIONS = 4
SLICES = 64
EXPERTS = 16
F_DEV = 256
CAP = 12
TOKENS = 4096


def levels(stream_key, shape, split, least, high):
    def one(dim, blocks):
        heights = jax.random.uniform(jax.random.fold_in(jax.random.fold_in(stream_key, 6), dim), (blocks,), jnp.float32, least / len(split), high / len(split))
        return jnp.repeat(jnp.exp(heights), shape[dim] // blocks).reshape((-1,) + (1,) * (len(shape) - dim - 1))

    gain = one(*split[0])
    for cut in split[1:]:
        gain = gain * one(*cut)
    return gain


def routed_block(key, own, number, rows, count, top, reach, lean):
    order = jax.random.permutation(key, count)
    crowded, usual = shares(count, rows * top, reach, lean, True), shares(count, rows * top, reach, lean, False)
    places = jnp.arange(count)

    def named(tallies, turn):
        used = int((tallies > 0).sum())
        fixed = max(1, used // 4)
        shifted = fixed + (places - fixed + turn * (used - fixed)) % max(1, count - fixed)
        return jnp.zeros((count,), jnp.int32).at[order[jnp.where(places < fixed, places, shifted)]].set(jnp.asarray(tallies, jnp.int32))

    tallies = jnp.where(number % 4 == 0, named(crowded, number // 4), named(usual, number - number // 4 - 1))
    mixed = jax.random.permutation(jax.random.fold_in(own, 3), count)
    donor, sink = mixed[0:count // 2 * 2:2], mixed[1:count // 2 * 2:2]
    room = jnp.minimum(tallies[donor] - 1, reach - tallies[sink]) // 2
    room = jnp.where((donor == order[0]) | (sink == order[0]) | (tallies[sink] == 0), 0, jnp.maximum(room, 0))
    shifted = jax.random.randint(jax.random.fold_in(own, 4), (count // 2,), 0, 1 << 20) % (room + 1)
    tallies = tallies.at[donor].add(-shifted).at[sink].add(shifted)
    labels = jnp.searchsorted(jnp.cumsum(tallies), jnp.arange(rows * top), side="right").astype(jnp.int32)
    grid = labels.reshape(top, rows).T
    grid = grid[jax.random.permutation(jax.random.fold_in(own, 1), rows)]
    turn = jax.random.randint(jax.random.fold_in(own, 2), (rows, 1), 0, top)
    return jnp.take_along_axis(grid, (jnp.arange(top)[None, :] + turn) % top, axis=1)


def shares(amount, total, limit, slope, full):
    portions = [(1 << 20) // math.isqrt(grade ** slope) + 1 for grade in range(1, amount + 1)]
    largest = limit if full else min(limit, max(-(-total // amount), total * portions[0] // sum(portions)))
    least = 1 if total - largest >= amount - 1 else 0
    counts, spare = [largest] + [least] * (amount - 1), total - largest - least * (amount - 1)
    while spare > 0:
        free = [i for i in range(1, amount) if counts[i] < largest] or [i for i in range(1, amount) if counts[i] < limit]
        whole, remaining = sum([portions[i] for i in free]), spare
        for i in free:
            extra = min(limit - counts[i], max(1, remaining * portions[i] // whole), spare)
            counts[i] = counts[i] + extra
            spare = spare - extra
    return np.array(counts)


def scatter_about(rng, dims, width, most, split=(), kind=jnp.bfloat16):
    factor_of = levels(rng, dims, split, -0.22, 0.18) if split else 1.0
    result = jax.random.normal(rng, dims, jnp.float32) * width * factor_of
    return jnp.minimum(jnp.maximum(result, -most), most).astype(kind)


def setup_inputs(seed: int = 0) -> dict:
    key_of = jax.random.split(jax.random.key(seed), 7)
    grad_out = scatter_about(key_of[0], (SECTIONS, 2, TOKENS, D), 0.5, 6.0, ((0, 4), (2, 64)))
    gate_probs = jnp.clip(jnp.exp(math.log(1.0) - 2.9996462 * jax.random.uniform(key_of[1], (SECTIONS, 2, TOKENS, TOP), jnp.float32) ** levels(key_of[1], (SECTIONS, 2, TOKENS, TOP), ((0, 4), (2, 64)), -0.2, 0.2)), 0.049804688, 1.0).astype(jnp.bfloat16)
    routes_keys = jax.random.split(jax.random.fold_in(key_of[2], 1), SECTIONS * 2 * TOKENS // TOK_DEV)
    routes_turns = jax.random.permutation(jax.random.fold_in(key_of[2], 3), SECTIONS * 2 * TOKENS // TOK_DEV)
    routes = jax.vmap(lambda own, number: routed_block(jax.random.fold_in(key_of[2], 2), own, number, TOK_DEV, EXPERTS, TOP, CAP, 2))(routes_keys, routes_turns).reshape((SECTIONS, 2, TOKENS, TOP))
    saved_preacts = scatter_about(key_of[3], (SECTIONS, 2, SLICES, SLICES, CAP, 2 * F_DEV), 1.0, 6.0, ((0, 4), (2, 64)))
    w_gate_up = scatter_about(key_of[4], (SECTIONS, SLICES, D, 2 * F_DEV), D ** -0.5, 0.09375, ((0, 4), (1, 64)))
    w_down = scatter_about(key_of[5], (SECTIONS, SLICES, F_DEV, D), FF ** -0.5, 0.1875, ((0, 4), (1, 64)))
    return dict(grad_out=grad_out, gate_probs=gate_probs, routes=routes, saved_preacts=saved_preacts, w_gate_up=w_gate_up, w_down=w_down)


def slot_targets(expert_ids, experts, capacity):
    flat_ids = expert_ids.reshape(-1)
    onehot = (flat_ids[:, None] == jnp.arange(experts, dtype=jnp.int32)[None, :]).astype(jnp.int32)
    before = jnp.cumsum(onehot, axis=0) - onehot
    slot_index = jnp.sum(before * onehot, axis=1)
    return (flat_ids * capacity + slot_index).astype(jnp.int32)


def pack_block(grad_rows, gate_rows, expert_ids, experts, capacity):
    tok_rows = grad_rows.shape[0]
    top_count = expert_ids.shape[1]
    targets = slot_targets(expert_ids, experts, capacity)
    matches = targets[:, None] == jnp.arange(experts * capacity, dtype=jnp.int32)[None, :]
    token_ids = jnp.repeat(jnp.arange(tok_rows, dtype=jnp.int32), top_count)
    source_row = jnp.sum(jnp.where(matches, token_ids[:, None], 0), axis=0).astype(jnp.int32)
    filled = jnp.any(matches, axis=0)
    gathered = jnp.where(filled[:, None], jnp.take(grad_rows, source_row, axis=0), jnp.zeros((), grad_rows.dtype))
    weights = jnp.sum(jnp.where(matches, gate_rows.reshape(-1)[:, None], jnp.zeros((), gate_rows.dtype)), axis=0).astype(gate_rows.dtype)
    return gathered.reshape(experts, capacity, -1), weights.reshape(experts, capacity), targets


def expert_slice(received, gate_vals, preacts, gate_up, down_proj):
    hidden_width = down_proj.shape[0]
    back_proj = lax.dot_general(received, down_proj, (((1,), (1,)), ((), ())), preferred_element_type=jnp.float32)
    gate_pre = preacts[:, :hidden_width].astype(jnp.float32)
    up_pre = preacts[:, hidden_width:].astype(jnp.float32)
    sigmoid_gate = 1.0 / (1.0 + jnp.exp(-gate_pre))
    activation = gate_pre * sigmoid_gate
    hidden = activation * up_pre
    prob_part = jnp.sum(hidden * back_proj, axis=1).astype(jnp.bfloat16)
    scale_vals = gate_vals.astype(jnp.float32)[:, None]
    d_hidden = scale_vals * back_proj
    d_gate = d_hidden * up_pre * sigmoid_gate * (1.0 + gate_pre * (1.0 - sigmoid_gate))
    d_up = d_hidden * activation
    d_both = jnp.concatenate([d_gate, d_up], axis=1).astype(jnp.bfloat16)
    grad_part = lax.dot_general(d_both, gate_up, (((1,), (1,)), ((), ())), preferred_element_type=jnp.float32).astype(jnp.bfloat16)
    scaled = (scale_vals * hidden).astype(jnp.bfloat16)
    weight_part = lax.dot_general(scaled, received, (((0,), (0,)), ((), ())), preferred_element_type=jnp.float32)
    return grad_part, prob_part, weight_part


def take_rows(table, targets):
    return jnp.take(table, targets, axis=0)


def reference(grad_out, gate_probs, routes, saved_preacts, w_gate_up, w_down):
    section_grads = []
    section_probs = []
    section_weights = []
    for section in range(SECTIONS):
        weight_sum = jnp.zeros((SLICES, F_DEV, D), jnp.float32)
        stretch_grads = []
        stretch_probs = []
        for stretch in range(2):
            grad_blocks = grad_out[section, stretch].reshape(SLICES, TOK_DEV, D)
            gate_blocks = gate_probs[section, stretch].reshape(SLICES, TOK_DEV, TOP)
            route_blocks = routes[section, stretch].reshape(SLICES, TOK_DEV, TOP)

            def pack_one(grad_rows, gate_rows, expert_ids):
                return pack_block(grad_rows, gate_rows, expert_ids, EXPERTS, CAP)

            rows_all, gates_all, targets = jax.vmap(pack_one)(grad_blocks, gate_blocks, route_blocks)

            def one_slice(item):
                index, preacts, gate_up, down_proj = item
                expert = index // SHARE
                received = lax.dynamic_index_in_dim(rows_all, expert, axis=1, keepdims=False)
                gate_vals = lax.dynamic_index_in_dim(gates_all, expert, axis=1, keepdims=False)
                grad_part, prob_part, weight_part = expert_slice(received.reshape(-1, D), gate_vals.reshape(-1), preacts.reshape(-1, 2 * F_DEV), gate_up, down_proj)
                return grad_part.reshape(SLICES, CAP, D), prob_part.reshape(SLICES, CAP), weight_part

            parts, prob_parts, weight_parts = lax.map(one_slice, (jnp.arange(SLICES, dtype=jnp.int32), saved_preacts[section, stretch], w_gate_up[section], w_down[section]))
            weight_sum = weight_sum + weight_parts
            folded = parts.astype(jnp.float32).reshape(EXPERTS, SHARE, SLICES, CAP, D).sum(axis=1)
            folded = lax.optimization_barrier(folded.astype(jnp.bfloat16)).astype(jnp.float32)
            folded = jnp.moveaxis(folded, 1, 0).reshape(SLICES, EXPERTS * CAP, D)
            prob_fold = prob_parts.astype(jnp.float32).reshape(EXPERTS, SHARE, SLICES, CAP).sum(axis=1)
            prob_fold = lax.optimization_barrier(prob_fold.astype(jnp.bfloat16)).astype(jnp.float32)
            prob_fold = jnp.moveaxis(prob_fold, 1, 0).reshape(SLICES, EXPERTS * CAP)
            token_grad = jax.vmap(take_rows)(folded, targets).reshape(TOKENS, TOP, D).sum(axis=1).astype(jnp.bfloat16)
            prob_grad = jax.vmap(take_rows)(prob_fold, targets).reshape(TOKENS, TOP)
            stretch_grads.append(token_grad)
            stretch_probs.append(prob_grad)
        section_grads.append(jnp.stack(stretch_grads))
        section_probs.append(jnp.stack(stretch_probs))
        section_weights.append(weight_sum.astype(jnp.bfloat16))
    token_grads = jnp.stack(section_grads)
    prob_grad = jnp.stack(section_probs)
    down_grad = jnp.stack(section_weights)
    downward = token_grads[:, 0]
    upward = token_grads[:, 1]
    zero_rows = jnp.zeros_like(downward[:1])
    from_above = jnp.concatenate([downward[1:], zero_rows], axis=0)
    from_below = jnp.concatenate([zero_rows, upward[:-1]], axis=0)
    return (from_above, from_below, prob_grad, down_grad)
```

```python
import functools

import jax
import jax.numpy as jnp
from jax import lax
from jax.experimental import pallas as pl
from jax.experimental.pallas import tpu as pltpu
from jax.sharding import Mesh, PartitionSpec as P

SHARE = 4
DEPTH = 2 * SHARE
CHUNKS = 4
HALF = 64
LANES = 128
META = 8
VMEM_LIMIT = 48 * 1024 * 1024

f32 = jnp.float32
bf16 = jnp.bfloat16


def shifted(block, distance):
    devices = range(lax.axis_size("section"))
    route = [(i - distance, i) for i in devices if i - distance in devices]
    return lax.ppermute(block, "section", route)


def slot_keys(meta, first, stride, count, capacity):
    ids = (first + stride * lax.broadcasted_iota(jnp.int32, (count, LANES), 0)).astype(f32)
    named = (meta[0:1, :] == ids) | (meta[1:2, :] == ids)
    row = lax.broadcasted_iota(jnp.int32, (LANES, LANES), 0)
    col = lax.broadcasted_iota(jnp.int32, (LANES, LANES), 1)
    earlier = (row < col) & (row // HALF == col // HALF)
    before = lax.dot_general(
        named.astype(f32).astype(bf16),
        earlier.astype(f32).astype(bf16),
        (((1,), (0,)), ((), ())),
        preferred_element_type=f32,
    )
    stretch = lax.broadcasted_iota(jnp.int32, (count, LANES), 1) // HALF
    return jnp.where(named, before + (stretch * capacity).astype(f32), -1.0)


def slot_matrix(meta, first, stride, count, capacity):
    keys = slot_keys(meta, first, stride, count, capacity)
    span = 2 * capacity
    slot = lax.broadcasted_iota(jnp.int32, (count, span, LANES), 1).astype(f32)
    hit = jnp.where(slot == keys[:, None, :], 1.0, 0.0)
    return hit.reshape(count * span, LANES).astype(bf16)


def pack_kernel(capacity, place, meta, rows, out):
    columns = out.shape[0]
    hits = slot_matrix(meta[0, 0], place[1], 2, columns, capacity)
    packed = jnp.dot(hits, rows[0], preferred_element_type=f32)
    out[:, 0] = packed.astype(bf16).reshape(columns, 2 * capacity, rows.shape[2])


def pack(place, meta, rows, columns, capacity):
    depth, tokens, width = rows.shape
    span = 2 * capacity
    return pl.pallas_call(
        functools.partial(pack_kernel, capacity),
        out_shape=jax.ShapeDtypeStruct((columns, depth, span, width), bf16),
        grid_spec=pltpu.PrefetchScalarGridSpec(
            num_scalar_prefetch=1,
            grid=(depth,),
            in_specs=[
                pl.BlockSpec((1, 1, META, LANES), lambda z, place: (place[0], z, 0, 0)),
                pl.BlockSpec((1, tokens, width), lambda z, place: (z, 0, 0)),
            ],
            out_specs=pl.BlockSpec((columns, 1, span, width), lambda z, place: (0, z, 0, 0)),
        ),
        compiler_params=pltpu.CompilerParams(vmem_limit_bytes=VMEM_LIMIT),
        name="pack_rows",
    )(place, meta, rows)


def fold_kernel(capacity, place, meta, rows, out):
    columns = rows.shape[0]
    hits = slot_matrix(meta[0, 0], place[1], 2, columns, capacity)
    flat = rows[:, 0].reshape(columns * 2 * capacity, rows.shape[3])
    total = lax.dot_general(hits, flat, (((0,), (0,)), ((), ())), preferred_element_type=f32)
    out[0] = total.astype(bf16)


def fold(place, meta, rows, capacity):
    columns, depth, span, width = rows.shape
    return pl.pallas_call(
        functools.partial(fold_kernel, capacity),
        out_shape=jax.ShapeDtypeStruct((depth, LANES, width), bf16),
        grid_spec=pltpu.PrefetchScalarGridSpec(
            num_scalar_prefetch=1,
            grid=(depth,),
            in_specs=[
                pl.BlockSpec((1, 1, META, LANES), lambda z, place: (place[0], z, 0, 0)),
                pl.BlockSpec((columns, 1, span, width), lambda z, place: (0, z, 0, 0)),
            ],
            out_specs=pl.BlockSpec((1, LANES, width), lambda z, place: (z, 0, 0)),
        ),
        compiler_params=pltpu.CompilerParams(vmem_limit_bytes=VMEM_LIMIT),
        name="fold_rows",
    )(place, meta, rows)


def weights_kernel(capacity, place, meta, preacts, scaled, gate_fac, up_fac, hidden):
    depth = meta.shape[1]
    span = 2 * capacity
    width = hidden.shape[1]
    columns = []
    for z in range(depth):
        block = meta[0, z]
        keys = slot_keys(block, place[2], 0, 8, capacity)[0:1]
        own = place[2].astype(f32)
        gates = jnp.where(block[0:1] == own, block[2:3], 0.0) + jnp.where(block[1:2] == own, block[3:4], 0.0)
        slot = lax.broadcasted_iota(jnp.int32, (span, LANES), 0).astype(f32)
        columns.append(jnp.sum(jnp.where(slot == keys, gates, 0.0), axis=1, keepdims=True))
    scale = jnp.concatenate(columns, axis=0)
    gate_pre = preacts[:, :width].astype(f32)
    up_pre = preacts[:, width:].astype(f32)
    sig = 1.0 / (1.0 + jnp.exp(-gate_pre))
    act = gate_pre * sig
    both = act * up_pre
    hidden[...] = both
    scaled[...] = (scale * both).astype(bf16)
    gate_fac[...] = scale * (up_pre * sig * (1.0 + gate_pre * (1.0 - sig)))
    up_fac[...] = scale * act


def slot_weights(place, meta, preacts, capacity):
    columns, depth = meta.shape[:2]
    rows = depth * 2 * capacity
    total, both = preacts.shape
    width = both // 2
    block = pl.BlockSpec((rows, width), lambda i, place: (i, 0))
    shape = functools.partial(jax.ShapeDtypeStruct, (total, width))
    return pl.pallas_call(
        functools.partial(weights_kernel, capacity),
        out_shape=[shape(bf16), shape(f32), shape(f32), shape(f32)],
        grid_spec=pltpu.PrefetchScalarGridSpec(
            num_scalar_prefetch=1,
            grid=(columns,),
            in_specs=[
                pl.BlockSpec((1, depth, META, LANES), lambda i, place: (i, 0, 0, 0)),
                pl.BlockSpec((rows, both), lambda i, place: (i, 0)),
            ],
            out_specs=[block] * 4,
        ),
        compiler_params=pltpu.CompilerParams(vmem_limit_bytes=VMEM_LIMIT),
        name="slot_weights",
    )(place, meta, preacts)


def shards(grad_out, gate_probs, routes, saved_preacts, w_gate_up, w_down):
    columns = lax.axis_size("column")
    depth = lax.axis_size("depth")
    capacity = saved_preacts.shape[4]
    span = 2 * capacity
    sources = columns * depth
    width = grad_out.shape[3]
    tokens = grad_out.shape[2]
    step = width // CHUNKS
    column = lax.axis_index("column")
    level = lax.axis_index("depth")
    half = level // SHARE
    own = 2 * column + half
    place = jnp.stack([column, half, own]).astype(jnp.int32)
    gate_up = w_gate_up[0, 0]
    down_proj = w_down[0, 0]

    picks = jnp.moveaxis(routes[0], 2, 0).reshape(2, 2 * tokens).astype(f32)
    gates = jnp.moveaxis(gate_probs[0], 2, 0).reshape(2, 2 * tokens).astype(f32)
    own_meta = jnp.concatenate([picks, gates, jnp.zeros((META - 4, 2 * tokens), f32)])
    meta = lax.all_gather(own_meta, ("column", "depth"), axis=0, tiled=False)
    meta = meta.reshape(columns, depth, META, LANES)

    rows_in = grad_out[0].reshape(2 * tokens, width)
    got = []
    back = None
    for c in range(CHUNKS):
        part = rows_in[:, c * step : (c + 1) * step]
        gathered = lax.all_gather(part, "depth", axis=0, tiled=False)
        sent = pack(place, meta, gathered, columns, capacity)
        got.append(
            lax.all_to_all(sent, "column", split_axis=0, concat_axis=0, tiled=True).reshape(
                sources * span, step
            )
        )
    preacts = jnp.concatenate([saved_preacts[0, 0, 0], saved_preacts[0, 1, 0]], axis=1)
    scaled, gate_fac, up_fac, hidden = slot_weights(
        place, meta, preacts.reshape(sources * span, -1), capacity
    )
    for c in range(CHUNKS):
        piece = lax.dot_general(
            got[c],
            down_proj[:, c * step : (c + 1) * step],
            (((1,), (1,)), ((), ())),
            preferred_element_type=f32,
        )
        back = piece if back is None else back + piece
    prob_part = jnp.sum(hidden * back, axis=1).astype(bf16)
    d_both = jnp.concatenate([back * gate_fac, back * up_fac], axis=1).astype(bf16)

    above, below, down_parts = [], [], []
    for c in range(CHUNKS):
        part = lax.dot_general(
            d_both,
            gate_up[c * step : (c + 1) * step],
            (((1,), (1,)), ((), ())),
            preferred_element_type=f32,
        ).astype(bf16)
        returned = lax.all_to_all(
            part.reshape(columns, depth, span, step), "column", split_axis=0, concat_axis=0, tiled=True
        )
        folded = fold(place, meta, returned, capacity)
        token_grad = lax.psum_scatter(folded, "depth", scatter_dimension=0, tiled=False)
        above.append(shifted(token_grad[:tokens], -1))
        below.append(shifted(token_grad[tokens:], 1))
    for c in range(CHUNKS):
        down_parts.append(
            lax.dot_general(
                scaled, got[c], (((0,), (0,)), ((), ())), preferred_element_type=f32
            ).astype(bf16)
        )

    prob_all = lax.all_gather(
        jnp.pad(prob_part, (0, 2048 - sources * span)).reshape(16, LANES), ("column", "depth"), axis=0, tiled=False
    ).reshape(sources, 2048)
    mine = lax.dynamic_slice(prob_all, (0, (column * depth + level) * span), (sources, span))
    group_prob = mine.astype(f32).reshape(sources // SHARE, SHARE, span).sum(axis=1)
    group_prob = lax.optimization_barrier(group_prob.astype(bf16)).astype(f32)
    keys = slot_keys(own_meta, 0, 1, sources // SHARE, capacity)
    slot = jnp.arange(span, dtype=jnp.int32).astype(f32)
    by_expert = jnp.sum(
        jnp.where(keys[:, None, :] == slot[None, :, None], group_prob[:, :, None], 0.0), axis=1
    )
    expert = jnp.arange(sources // SHARE, dtype=jnp.int32).astype(f32)
    prob_grad = jnp.sum(
        jnp.where(picks[:, None, :] == expert[None, :, None], by_expert[None], 0.0), axis=1
    )
    prob_grad = jnp.moveaxis(prob_grad.reshape(2, 2, tokens), 0, 2)
    return (
        jnp.concatenate(above, axis=1)[None],
        jnp.concatenate(below, axis=1)[None],
        prob_grad[None],
        jnp.concatenate(down_parts, axis=1)[None, None],
    )


def solution(mesh):
    sections, slices = mesh.devices.shape
    grid = Mesh(mesh.devices.reshape(sections, slices // DEPTH, DEPTH), ("section", "column", "depth"))
    spread = ("column", "depth")
    in_specs = (
        P("section", None, spread, None),
        P("section", None, spread, None),
        P("section", None, spread, None),
        P("section", None, spread, None, None, None),
        P("section", spread, None, None),
        P("section", spread, None, None),
    )
    out_specs = (
        P("section", spread, None),
        P("section", spread, None),
        P("section", None, spread, None),
        P("section", spread, None, None),
    )
    return jax.shard_map(shards, mesh=grid, in_specs=in_specs, out_specs=out_specs, check_vma=False)
```

```python
import functools

import jax
import jax.numpy as jnp
from jax import lax
from jax.experimental import pallas as pl
from jax.experimental.pallas import tpu as pltpu
from jax.sharding import Mesh, PartitionSpec as P

SHARE = 4
DEPTH = 2 * SHARE
WIDTHS = (512, 1024, 1024, 1024)
EXTRA = 128
HALF = 64
LANES = 128
META = 16
VMEM_LIMIT = 48 * 1024 * 1024

f32 = jnp.float32
bf16 = jnp.bfloat16


def shifted(block, distance):
    devices = range(lax.axis_size("section"))
    route = [(i - distance, i) for i in devices if i - distance in devices]
    return lax.ppermute(block, "section", route)


def slot_hits(meta, first, stride, count, capacity):
    ids = (first + stride * lax.broadcasted_iota(jnp.int32, (count, LANES), 0)).astype(f32)
    named = (meta[0:1] == ids) | (meta[1:2] == ids)
    row = lax.broadcasted_iota(jnp.int32, (LANES, LANES), 0)
    col = lax.broadcasted_iota(jnp.int32, (LANES, LANES), 1)
    earlier = (row < col) & (row // HALF == col // HALF)
    before = lax.dot_general(
        named.astype(f32).astype(bf16),
        earlier.astype(f32).astype(bf16),
        (((1,), (0,)), ((), ())),
        preferred_element_type=f32,
    )
    stretch = lax.broadcasted_iota(jnp.int32, (count, LANES), 1) // HALF
    keys = jnp.where(named, before + (stretch * capacity).astype(f32), -1.0)
    slot = lax.broadcasted_iota(jnp.int32, (count, 2 * capacity, LANES), 1).astype(f32)
    return jnp.where(slot == keys[:, None, :], 1.0, 0.0), ids


def flat(hits):
    return hits.reshape(-1, LANES).astype(bf16)


def pack_kernel(capacity, width, place, meta_rows, rows, out):
    columns = out.shape[0]
    meta = meta_rows[0].astype(f32)
    hits, ids = slot_hits(meta, place[0], 2, columns, capacity)
    packed = jnp.dot(flat(hits), rows[0, :LANES], preferred_element_type=f32)
    out[:, 0, :, :width] = packed.astype(bf16).reshape(columns, 2 * capacity, width)
    if out.shape[3] > width:
        gates = jnp.where(meta[0:1] == ids, meta[2:3], 0.0) + jnp.where(meta[1:2] == ids, meta[3:4], 0.0)
        scale = jnp.sum(hits * gates[:, None, :], axis=2, keepdims=True)
        out[:, 0, :, width:] = jnp.broadcast_to(scale, (columns, 2 * capacity, EXTRA)).astype(bf16)


def pack(place, tagged, rows, columns, capacity, extra):
    depth, tokens, width = rows.shape
    span = 2 * capacity
    return pl.pallas_call(
        functools.partial(pack_kernel, capacity, width),
        out_shape=jax.ShapeDtypeStruct((columns, depth, span, width + extra), bf16),
        grid_spec=pltpu.PrefetchScalarGridSpec(
            num_scalar_prefetch=1,
            grid=(depth,),
            in_specs=[
                pl.BlockSpec((1, META, LANES), lambda z, place: (z, LANES // META, 0)),
                pl.BlockSpec((1, tokens, width), lambda z, place: (z, 0, 0)),
            ],
            out_specs=pl.BlockSpec((columns, 1, span, width + extra), lambda z, place: (0, z, 0, 0)),
        ),
        compiler_params=pltpu.CompilerParams(vmem_limit_bytes=VMEM_LIMIT),
        name="pack_rows",
    )(place, tagged, rows)


def fold_kernel(capacity, width, place, meta_rows, rows, *rest):
    out = rest[-1]
    columns = rows.shape[0]
    meta = meta_rows[0].astype(f32)
    hits, ids = slot_hits(meta, place[0], 2, columns, capacity)
    table = rows[:, 0].reshape(columns * 2 * capacity, rows.shape[3])
    contract = (((0,), (0,)), ((), ()))
    total = lax.dot_general(flat(hits), table[:, :width], contract, preferred_element_type=f32)
    out[0, :, :width] = total.astype(bf16)
    if out.shape[2] > width:
        first = flat(hits * jnp.where(meta[0:1] == ids, 1.0, 0.0)[:, None, :])
        second = flat(hits * jnp.where(meta[1:2] == ids, 1.0, 0.0)[:, None, :])
        parts = table[:, width:]
        low = lax.dot_general(first, parts, contract, preferred_element_type=f32)
        high = lax.dot_general(second, parts, contract, preferred_element_type=f32)
        lane = lax.broadcasted_iota(jnp.int32, (LANES, EXTRA), 1)
        out[0, :, width:] = jnp.where(lane < HALF, low, high).astype(bf16)


def fold(place, tagged, rows, capacity, extra, earlier=()):
    columns, depth, span, width = rows.shape
    return pl.pallas_call(
        functools.partial(fold_kernel, capacity, width - extra),
        out_shape=jax.ShapeDtypeStruct((depth, LANES, width), bf16),
        grid_spec=pltpu.PrefetchScalarGridSpec(
            num_scalar_prefetch=1,
            grid=(depth,),
            in_specs=[
                pl.BlockSpec((1, META, LANES), lambda z, place: (z, LANES // META, 0)),
                pl.BlockSpec((columns, 1, span, width), lambda z, place: (0, z, 0, 0)),
            ]
            + [pl.BlockSpec(memory_space=pl.ANY)] * len(earlier),
            out_specs=pl.BlockSpec((1, LANES, width), lambda z, place: (z, 0, 0)),
        ),
        compiler_params=pltpu.CompilerParams(vmem_limit_bytes=VMEM_LIMIT),
        name="fold_rows",
    )(place, tagged, rows, *earlier)


def weights_kernel(scales, preacts, scaled, gate_fac, up_fac, hidden):
    width = hidden.shape[1]
    scale = scales[:, 0:1].astype(f32)
    gate_pre = preacts[:, :width].astype(f32)
    up_pre = preacts[:, width:].astype(f32)
    sig = 1.0 / (1.0 + jnp.exp(-gate_pre))
    act = gate_pre * sig
    both = act * up_pre
    hidden[...] = both
    scaled[...] = (scale * both).astype(bf16)
    gate_fac[...] = scale * (up_pre * sig * (1.0 + gate_pre * (1.0 - sig)))
    up_fac[...] = scale * act


def slot_weights(received, preacts, steps):
    total, both = preacts.shape
    width = both // 2
    rows = total // steps
    last = received.shape[1] // EXTRA - 1
    block = pl.BlockSpec((rows, width), lambda i: (i, 0))
    shape = functools.partial(jax.ShapeDtypeStruct, (total, width))
    return pl.pallas_call(
        weights_kernel,
        out_shape=[shape(bf16), shape(f32), shape(f32), shape(f32)],
        grid=(steps,),
        in_specs=[
            pl.BlockSpec((rows, EXTRA), lambda i: (i, last)),
            pl.BlockSpec((rows, both), lambda i: (i, 0)),
        ],
        out_specs=[block] * 4,
        compiler_params=pltpu.CompilerParams(vmem_limit_bytes=VMEM_LIMIT),
        name="slot_weights",
    )(received, preacts)


NT = (((1,), (1,)), ((), ()))


def slice_grad(both, gate_up, out):
    grad = lax.dot_general(both, gate_up, NT, preferred_element_type=f32)
    out[0, :, :, : gate_up.shape[0]] = grad.astype(bf16).reshape(out.shape[1], out.shape[2], gate_up.shape[0])


def middle_kernel(last, down_proj, back, gate_fac, up_fac, hidden, gate_up, both, probs, out):
    total = back[...] + lax.dot_general(last[...], down_proj[...], NT, preferred_element_type=f32)
    part = jnp.sum(hidden[...] * total, axis=1, keepdims=True)
    probs[...] = jnp.broadcast_to(part, probs.shape).astype(bf16)
    half = total.shape[1]
    both[:, :half] = (total * gate_fac[...]).astype(bf16)
    both[:, half:] = (total * up_fac[...]).astype(bf16)
    slice_grad(both[...], gate_up[...], out)


def middle(last, down_proj, piece, back, gate_fac, up_fac, hidden, gate_up, block, width, grid_shape):
    columns, depth, span = grid_shape
    rows = depth * span
    total, half = back.shape
    full = gate_up.shape[1]
    wide = pl.BlockSpec((rows, half), lambda i: (i, 0))
    return pl.pallas_call(
        middle_kernel,
        out_shape=[
            jax.ShapeDtypeStruct((total, full), bf16),
            jax.ShapeDtypeStruct((total, EXTRA), bf16),
            jax.ShapeDtypeStruct((columns, depth, span, width), bf16),
        ],
        grid=(columns,),
        in_specs=[
            pl.BlockSpec((rows, last.shape[1]), lambda i: (i, 0)),
            pl.BlockSpec((half, last.shape[1]), lambda i: (0, piece)),
            wide,
            wide,
            wide,
            wide,
            pl.BlockSpec((width, full), lambda i: (block, 0)),
        ],
        out_specs=[
            pl.BlockSpec((rows, full), lambda i: (i, 0)),
            pl.BlockSpec((rows, EXTRA), lambda i: (i, 0)),
            pl.BlockSpec((1, depth, span, width), lambda i: (i, 0, 0, 0)),
        ],
        compiler_params=pltpu.CompilerParams(vmem_limit_bytes=VMEM_LIMIT),
        name="middle",
    )(last, down_proj, back, gate_fac, up_fac, hidden, gate_up)


def grad_kernel(both, gate_up, probs, *rest):
    out = rest[-1]
    slice_grad(both[...], gate_up[...], out)
    width = gate_up.shape[0]
    if out.shape[3] > width:
        out[0, :, :, width:] = probs[...].reshape(out.shape[1], out.shape[2], EXTRA)


def back_part(both, gate_up, probs, block, width, extra, grid_shape, earlier):
    columns, depth, span = grid_shape
    rows = depth * span
    full = gate_up.shape[1]
    return pl.pallas_call(
        grad_kernel,
        out_shape=jax.ShapeDtypeStruct((columns, depth, span, width + extra), bf16),
        grid=(columns,),
        in_specs=[
            pl.BlockSpec((rows, full), lambda i: (i, 0)),
            pl.BlockSpec((width, full), lambda i: (block, 0)),
            pl.BlockSpec((rows, EXTRA), lambda i: (i, 0)),
        ]
        + [pl.BlockSpec(memory_space=pl.ANY)] * len(earlier),
        out_specs=pl.BlockSpec((1, depth, span, width + extra), lambda i: (i, 0, 0, 0)),
        compiler_params=pltpu.CompilerParams(vmem_limit_bytes=VMEM_LIMIT),
        name="slice_grad",
    )(both, gate_up, probs, *earlier)


def exchange(block):
    return lax.all_to_all(block, "column", split_axis=0, concat_axis=0, tiled=True)


def shards(grad_out, gate_probs, routes, saved_preacts, w_gate_up, w_down):
    columns = lax.axis_size("column")
    depth = lax.axis_size("depth")
    capacity = saved_preacts.shape[4]
    span = 2 * capacity
    slots = columns * depth * span
    grid_shape = (columns, depth, span)
    width = grad_out.shape[3]
    tokens = grad_out.shape[2]
    starts = [sum(WIDTHS[1:])] + [sum(WIDTHS[1:c]) for c in range(1, len(WIDTHS))]
    bounds = [(low, low + size) for low, size in zip(starts, WIDTHS)]
    half = lax.axis_index("depth") // SHARE
    place = half.astype(jnp.int32).reshape(1)
    gate_up = w_gate_up[0, 0]
    down_proj = w_down[0, 0]

    picks = jnp.moveaxis(routes[0], 2, 0).reshape(2, 2 * tokens).astype(bf16)
    gates = jnp.moveaxis(gate_probs[0], 2, 0).reshape(2, 2 * tokens)
    tags = jnp.pad(jnp.concatenate([picks, gates]), ((0, META - 4), (0, WIDTHS[0] - 2 * tokens)))

    rows_in = grad_out[0].reshape(2 * tokens, width)
    got = []
    tagged = None
    for c, (low, high) in enumerate(bounds):
        part = rows_in[:, low:high]
        if c == 0:
            part = jnp.concatenate([part, tags])
        gathered = lax.all_gather(part, "depth", axis=0, tiled=False)
        tagged = gathered if c == 0 else tagged
        sent = pack(place, tagged, gathered, columns, capacity, EXTRA if c == 0 else 0)
        got.append(exchange(sent).reshape(slots, -1))
    preacts = jnp.concatenate([saved_preacts[0, 0, 0], saved_preacts[0, 1, 0]], axis=1)
    scaled, gate_fac, up_fac, hidden = slot_weights(got[0], preacts.reshape(slots, -1), columns)
    back = None
    for c in range(len(bounds) - 1):
        low, high = bounds[c]
        piece = lax.dot_general(
            got[c][:, : high - low], down_proj[:, low:high], NT, preferred_element_type=f32
        )
        back = piece if back is None else back + piece

    def down_slice(c):
        low, high = bounds[c]
        return lax.dot_general(
            scaled, got[c][:, : high - low], (((0,), (0,)), ((), ())), preferred_element_type=f32
        ).astype(bf16)

    order = list(range(1, len(bounds))) + [0]
    last = len(bounds) - 1
    both, probs, sending = middle(
        got[last],
        down_proj,
        bounds[last][0] // WIDTHS[last],
        back,
        gate_fac,
        up_fac,
        hidden,
        gate_up,
        bounds[order[0]][0] // WIDTHS[order[0]],
        WIDTHS[order[0]],
        grid_shape,
    )
    downs, moved, folded = {}, {}, {}
    for n, c in enumerate(order):
        returned = exchange(sending)
        if n + 1 < len(order):
            following = order[n + 1]
            earlier = []
            if n >= 1:
                downs[order[n - 1]] = down_slice(order[n - 1])
                earlier = [folded[order[n - 1]], downs[order[n - 1]]]
            following_rows = back_part(
                both,
                gate_up,
                probs,
                bounds[following][0] // WIDTHS[following],
                WIDTHS[following],
                EXTRA if following == 0 else 0,
                grid_shape,
                earlier,
            )
            earlier = [following_rows]
            sending = following_rows
        else:
            downs[order[n - 1]] = down_slice(order[n - 1])
            downs[c] = down_slice(c)
            down_grad = jnp.concatenate([downs[k] for k in order], axis=1)
            earlier = [down_grad, folded[order[n - 1]]] + [piece for k in order[: n - 1] for piece in moved[k]]
        folded[c] = fold(place, tagged, returned, capacity, EXTRA if c == 0 else 0, earlier)
        reduced = lax.psum_scatter(folded[c], "depth", scatter_dimension=0, tiled=False)
        moved[c] = (
            shifted(reduced[:tokens, : WIDTHS[c]], -1),
            shifted(reduced[tokens:, : WIDTHS[c]], 1),
        )
    prob_grad = reduced[:, WIDTHS[0] :].reshape(2, tokens, 2, HALF)[:, :, :, 0].astype(f32)
    return (
        jnp.concatenate([moved[c][0] for c in order], axis=1)[None],
        jnp.concatenate([moved[c][1] for c in order], axis=1)[None],
        prob_grad[None],
        down_grad[None, None],
    )


def solution(mesh):
    sections, slices = mesh.devices.shape
    grid = Mesh(mesh.devices.reshape(sections, slices // DEPTH, DEPTH), ("section", "column", "depth"))
    spread = ("column", "depth")
    in_specs = (
        P("section", None, spread, None),
        P("section", None, spread, None),
        P("section", None, spread, None),
        P("section", None, spread, None, None, None),
        P("section", spread, None, None),
        P("section", spread, None, None),
    )
    out_specs = (
        P("section", spread, None),
        P("section", spread, None),
        P("section", None, spread, None),
        P("section", spread, None, None),
    )
    return jax.shard_map(shards, mesh=grid, in_specs=in_specs, out_specs=out_specs, check_vma=False)
```

```python
import functools

import jax
import jax.numpy as jnp
from jax import lax
from jax.experimental import pallas as pl
from jax.experimental.pallas import tpu as pltpu
from jax.sharding import Mesh, PartitionSpec as P

SHARE = 4
DEPTH = 2 * SHARE
GROUPS = ((0,), (-1, 1), (-2, 2), (-3, 3), (-4,))
EXTRA = 128
HALF = 64
LANES = 128
META = 8
TILE = 512
VMEM_LIMIT = 56 * 1024 * 1024

f32 = jnp.float32
bf16 = jnp.bfloat16
NT = (((1,), (1,)), ((), ()))
TN = (((0,), (0,)), ((), ()))


def tags(rows):
    meta = rows[LANES : LANES + META, : 4 * LANES].astype(f32)
    return [meta[0:1, k * LANES : (k + 1) * LANES] for k in range(4)]


def slot_hits(picks, half, count, capacity):
    ids = (half + 2 * lax.broadcasted_iota(jnp.int32, (count, LANES), 0)).astype(f32)
    named = (picks[0] == ids) | (picks[1] == ids)
    row = lax.broadcasted_iota(jnp.int32, (LANES, LANES), 0)
    col = lax.broadcasted_iota(jnp.int32, (LANES, LANES), 1)
    earlier = (row < col) & (row // HALF == col // HALF)
    before = jnp.dot(
        named.astype(f32).astype(bf16), earlier.astype(f32).astype(bf16), preferred_element_type=f32
    )
    stretch = lax.broadcasted_iota(jnp.int32, (count, LANES), 1) // HALF
    keys = jnp.where(named, before + (stretch * capacity).astype(f32), -1.0)
    slot = lax.broadcasted_iota(jnp.int32, (count, 2 * capacity, LANES), 1).astype(f32)
    return jnp.where(slot == keys[:, None, :], 1.0, 0.0), ids


def flat(hits):
    return hits.reshape(-1, LANES).astype(bf16)


def tiles(width):
    return [slice(low, low + TILE) for low in range(0, width, TILE)]


def params():
    return pltpu.CompilerParams(vmem_limit_bytes=VMEM_LIMIT)


SMEM = pl.BlockSpec(memory_space=pltpu.SMEM)
VMEM = pl.BlockSpec(memory_space=pltpu.VMEM)
ANY = pl.BlockSpec(memory_space=pl.ANY)


def pack_kernel(capacity, count, tagged, width, place, *refs):
    out = refs[-1]
    columns = out.shape[0]
    for m in range(count):
        rows = refs[m]
        hits, _ = slot_hits(tags(rows), place[0], columns, capacity)
        ones = flat(hits)
        for tile in tiles(width):
            packed = jnp.dot(ones, rows[:LANES, tile], preferred_element_type=f32)
            out[:, m, :, tile] = packed.astype(bf16).reshape(columns, 2 * capacity, TILE)
    if out.shape[3] > width:
        lane = lax.broadcasted_iota(jnp.int32, (columns, 2 * capacity, EXTRA), 2)
        scales = jnp.zeros((columns, 2 * capacity, EXTRA), f32)
        for k, rows in enumerate(refs[count : count + tagged]):
            meta = rows[:, :].astype(f32)
            picks = [meta[0:1, i * LANES : (i + 1) * LANES] for i in range(4)]
            hits, ids = slot_hits(picks, place[0], columns, capacity)
            gates = jnp.where(picks[0] == ids, picks[2], 0.0) + jnp.where(picks[1] == ids, picks[3], 0.0)
            scale = jnp.sum(hits * gates[:, None, :], axis=2, keepdims=True)
            scales = jnp.where(lane == k, scale, scales)
        out[:, 0, :, width:] = scales.astype(bf16)


def pack(place, arrivals, columns, capacity, tagged=(), earlier=()):
    width = arrivals[0].shape[1]
    extra = EXTRA if tagged else 0
    only_tags = pl.BlockSpec((META, 4 * LANES), lambda i: (LANES // META, 0))
    return pl.pallas_call(
        functools.partial(pack_kernel, capacity, len(arrivals), len(tagged), width),
        out_shape=jax.ShapeDtypeStruct((columns, len(arrivals), 2 * capacity, width + extra), bf16),
        grid=(1,),
        in_specs=[SMEM] + [VMEM] * len(arrivals) + [only_tags] * len(tagged) + [ANY] * len(earlier),
        out_specs=VMEM,
        compiler_params=params(),
        name="pack_rows",
    )(place, *arrivals, *tagged, *earlier)


def expert_parts(rows, preacts, down_proj):
    width = down_proj.shape[1]
    half = down_proj.shape[0]
    back = lax.dot_general(rows, down_proj, NT, preferred_element_type=f32)
    gate_pre = preacts[:, :half].astype(f32)
    up_pre = preacts[:, half:].astype(f32)
    sig = 1.0 / (1.0 + jnp.exp(-gate_pre))
    act = gate_pre * sig
    hidden = act * up_pre
    part = jnp.sum(hidden * back, axis=1, keepdims=True)
    gate_side = back * up_pre * sig * (1.0 + gate_pre * (1.0 - sig))
    return gate_side, back * act, hidden, part


def prepare_kernel(width, place, rows, preacts, down_proj, sides, hidden, parts):
    slots = sides.shape[1]
    half = hidden.shape[2]
    table = rows[:, 0, :, :width].reshape(slots, width)
    pre = preacts[:, 0].reshape(slots, 2 * half)
    gate_side, up_side, hid, part = expert_parts(table, pre, down_proj[...])
    sides[0, :, :half] = gate_side
    sides[0, :, half:] = up_side
    hidden[0] = hid
    parts[0] = jnp.broadcast_to(part, (slots, EXTRA))


def prepare(place, received, preacts, down_proj):
    columns, count, span = received.shape[:3]
    half, width = down_proj.shape
    slots = columns * span
    block = lambda m, place: (m, 0, 0)
    return pl.pallas_call(
        functools.partial(prepare_kernel, width),
        out_shape=[
            jax.ShapeDtypeStruct((count, slots, 2 * half), f32),
            jax.ShapeDtypeStruct((count, slots, half), f32),
            jax.ShapeDtypeStruct((count, slots, EXTRA), f32),
        ],
        grid_spec=pltpu.PrefetchScalarGridSpec(
            num_scalar_prefetch=1,
            grid=(count,),
            in_specs=[
                pl.BlockSpec((columns, 1, span, width), lambda m, place: (0, m, 0, 0)),
                pl.BlockSpec((columns, 1, span, 2 * half), lambda m, place: (0, place[1 + m], 0, 0)),
                pl.BlockSpec((half, width), lambda m, place: (0, 0)),
            ],
            out_specs=[
                pl.BlockSpec((1, slots, 2 * half), block),
                pl.BlockSpec((1, slots, half), block),
                pl.BlockSpec((1, slots, EXTRA), block),
            ],
        ),
        compiler_params=params(),
        name="prepare",
    )(place, received, preacts, down_proj)


def turn_kernel(count, place, received, preacts, down_proj, gate_up, *refs):
    others, hidden, out = refs[:-2], refs[-2], refs[-1]
    half, width = down_proj.shape
    columns, _, span, _ = received.shape
    slots = columns * span
    table = received[:, 0, :, :width].reshape(slots, width)
    scales = received[:, 0, :, width:].astype(f32).reshape(slots, EXTRA)
    gate_side, up_side, hid, part = expert_parts(table, preacts[:, 0].reshape(slots, 2 * half), down_proj[...])
    hidden[0] = hid
    scale = scales[:, count - 1 : count]
    both = jnp.concatenate([scale * gate_side, scale * up_side], axis=1).astype(bf16)
    for tile in tiles(width):
        grad = lax.dot_general(both, gate_up[tile, :], NT, preferred_element_type=f32)
        out[:, 0, :, tile] = grad.astype(bf16).reshape(columns, span, TILE)
    lane = lax.broadcasted_iota(jnp.int32, (slots, EXTRA), 1)
    parts = jnp.where(lane == count - 1, part, 0.0)
    k = 0
    for group in others:
        for m in range(group.shape[0]):
            parts = jnp.where(lane == k, group[m], parts)
            k += 1
    out[:, 0, :, width:] = parts.astype(bf16).reshape(columns, span, EXTRA)


def turn(place, received, preacts, down_proj, gate_up, parts):
    columns, _, span, wide = received.shape
    half, width = down_proj.shape
    slots = columns * span
    count = 1 + sum(p.shape[0] for p in parts)
    return pl.pallas_call(
        functools.partial(turn_kernel, count),
        out_shape=[
            jax.ShapeDtypeStruct((1, slots, half), f32),
            jax.ShapeDtypeStruct((columns, 1, span, wide), bf16),
        ],
        grid_spec=pltpu.PrefetchScalarGridSpec(
            num_scalar_prefetch=1,
            grid=(1,),
            in_specs=[
                VMEM,
                pl.BlockSpec((columns, 1, span, 2 * half), lambda m, place: (0, place[1], 0, 0)),
                VMEM,
                VMEM,
            ]
            + [VMEM] * len(parts),
            out_specs=[VMEM, VMEM],
        ),
        compiler_params=params(),
        name="turn",
    )(place, received, preacts, down_proj, gate_up, *parts)


def grad_kernel(first, sides, last, gate_up, *rest):
    out = rest[-1]
    width = gate_up.shape[0]
    columns, _, span, _ = out.shape
    slots = columns * span
    scales = last[:, 0].reshape(slots, EXTRA).astype(f32)
    lane = lax.broadcasted_iota(jnp.int32, (slots, EXTRA), 1)
    index = first + pl.program_id(0)
    scale = jnp.sum(jnp.where(lane == index, scales, 0.0), axis=1, keepdims=True)
    both = (scale * sides[0]).astype(bf16)
    for tile in tiles(width):
        grad = lax.dot_general(both, gate_up[tile, :], NT, preferred_element_type=f32)
        out[:, 0, :, tile] = grad.astype(bf16).reshape(columns, span, TILE)


def slice_grad(first, sides, last, gate_up, earlier):
    count, slots, full = sides.shape
    columns, _, span, wide = last.shape
    width = gate_up.shape[0]
    return pl.pallas_call(
        functools.partial(grad_kernel, first),
        out_shape=jax.ShapeDtypeStruct((columns, count, span, width), bf16),
        grid=(count,),
        in_specs=[
            pl.BlockSpec((1, slots, full), lambda m: (m, 0, 0)),
            pl.BlockSpec((columns, 1, span, EXTRA), lambda m: (0, 0, 0, width // EXTRA)),
            pl.BlockSpec((width, full), lambda m: (0, 0)),
        ]
        + [ANY] * len(earlier),
        out_specs=pl.BlockSpec((columns, 1, span, width), lambda m: (0, m, 0, 0)),
        compiler_params=params(),
        name="slice_grad",
    )(sides, last, gate_up, *earlier)


def down_kernel(groups, last, *refs):
    rows, hidden, out, scaled = refs[:groups], refs[groups : 2 * groups], refs[-2], refs[-1]
    slots = hidden[0].shape[1]

    @pl.when(pl.program_id(0) == 0)
    def _():
        scales = last[:, 0].reshape(slots, EXTRA).astype(f32)
        k = 0
        for group in hidden:
            for m in range(group.shape[0]):
                scaled[k * slots : (k + 1) * slots] = (scales[:, k : k + 1] * group[m]).astype(bf16)
                k += 1

    total = jnp.zeros(out.shape, f32)
    k = 0
    for group in rows:
        for m in range(group.shape[1]):
            table = group[:, m].reshape(slots, out.shape[1])
            part = scaled[k * slots : (k + 1) * slots]
            total += lax.dot_general(part, table, TN, preferred_element_type=f32)
            k += 1
    out[...] = total.astype(bf16)


def down_grads(received, hidden, width):
    last = received[-1]
    columns, _, span, _ = last.shape
    count = sum(h.shape[0] for h in hidden)
    slots, half = hidden[0].shape[1:]
    return pl.pallas_call(
        functools.partial(down_kernel, len(received)),
        out_shape=jax.ShapeDtypeStruct((half, width), bf16),
        grid=(width // TILE,),
        in_specs=[pl.BlockSpec((columns, 1, span, EXTRA), lambda i: (0, 0, 0, width // EXTRA))]
        + [pl.BlockSpec((columns, g.shape[1], span, TILE), lambda i: (0, 0, 0, i)) for g in received]
        + [pl.BlockSpec(h.shape, lambda i: (0, 0, 0)) for h in hidden],
        out_specs=pl.BlockSpec((half, TILE), lambda i: (0, i)),
        scratch_shapes=[pltpu.VMEM((count * slots, half), bf16)],
        compiler_params=params(),
        name="down_grads",
    )(last, *received, *hidden)


def fold_kernel(capacity, first, count, coming, final, place, parts, *refs):
    returned = refs[0]
    metas = refs[1 : 1 + count]
    incoming = refs[1 + count : 1 + count + coming]
    outs = refs[-3:] if final else refs[-count:]
    columns, _, span, _ = returned.shape
    slots = columns * span
    table = parts[:, 0].astype(f32)
    for m in range(count):
        meta = metas[m][:, :].astype(f32)
        picks = [meta[0:1, i * LANES : (i + 1) * LANES] for i in range(4)]
        hits, ids = slot_hits(picks, place[0], columns, capacity)
        ones = flat(hits)
        added = list(incoming) if final else list(incoming[m : m + 1])
        for tile in tiles(returned.shape[3] // TILE * TILE):
            rows = returned[:, m, :, tile].reshape(slots, TILE)
            total = lax.dot_general(ones, rows, TN, preferred_element_type=f32)
            for other in added:
                total = total + other[:LANES, tile].astype(f32)
            total = total.astype(bf16)
            if final:
                outs[0][:, tile] = total[:HALF]
                outs[1][:, tile] = total[HALF:]
            else:
                outs[m][:LANES, tile] = total
        values = hits * table[:, :, first + m : first + m + 1]
        for k in range(2):
            named = jnp.where(picks[k] == ids, 1.0, 0.0)[:, None, :]
            line = jnp.sum(jnp.sum(values * named, axis=1), axis=0, keepdims=True)
            lanes = slice(k * LANES, (k + 1) * LANES)
            for other in added:
                line = line + other[LANES : LANES + META, lanes].astype(f32)[0:1]
            if final:
                outs[2][:, lanes] = jnp.broadcast_to(line, (META, LANES))
            else:
                outs[m][LANES : LANES + META, lanes] = jnp.broadcast_to(line, (META, LANES)).astype(bf16)


def fold(place, first, parts, returned, arrivals, incoming, capacity, final, earlier=()):
    columns, count, span, _ = returned.shape
    width = arrivals[0].shape[1]
    only_tags = pl.BlockSpec((META, 4 * LANES), lambda i: (LANES // META, 0))
    if final:
        shapes = [jax.ShapeDtypeStruct((HALF, width), bf16)] * 2
        shapes.append(jax.ShapeDtypeStruct((META, 2 * LANES), f32))
    else:
        shapes = [jax.ShapeDtypeStruct((LANES + META, width), bf16)] * count
    return pl.pallas_call(
        functools.partial(fold_kernel, capacity, first, count, len(incoming), final),
        out_shape=shapes,
        grid=(1,),
        in_specs=[SMEM, pl.BlockSpec((columns, 1, span, EXTRA), lambda i: (0, 0, 0, width // EXTRA)), VMEM]
        + [only_tags] * count
        + [VMEM] * len(incoming)
        + [ANY] * len(earlier),
        out_specs=[VMEM] * len(shapes),
        compiler_params=params(),
        name="fold_rows",
    )(place, parts, returned, *arrivals, *incoming, *earlier)


def exchange(block):
    return lax.all_to_all(block, "column", split_axis=0, concat_axis=0, tiled=True)


def hop(block, distance):
    return lax.ppermute(block, "depth", [(i, (i + distance) % DEPTH) for i in range(DEPTH)])


def shifted(block, distance):
    devices = range(lax.axis_size("section"))
    route = [(i - distance, i) for i in devices if i - distance in devices]
    return lax.ppermute(block, "section", route)


def shards(grad_out, gate_probs, routes, saved_preacts, w_gate_up, w_down):
    columns = lax.axis_size("column")
    capacity = saved_preacts.shape[4]
    span = 2 * capacity
    width = grad_out.shape[3]
    tokens = grad_out.shape[2]
    level = lax.axis_index("depth")
    half = level // SHARE
    gate_up = w_gate_up[0, 0]
    down_proj = w_down[0, 0]

    def place(group):
        where = [half] + [(level + DEPTH + offset) % DEPTH for offset in group]
        return jnp.stack(where).astype(jnp.int32)

    picks = jnp.moveaxis(routes[0], 2, 0).reshape(1, 4 * tokens).astype(bf16)
    gates = jnp.moveaxis(gate_probs[0], 2, 0).reshape(1, 4 * tokens)
    line = jnp.concatenate([picks, gates], axis=1)
    own = jnp.concatenate(
        [
            grad_out[0].reshape(2 * tokens, width),
            jnp.pad(line, ((0, META - 1), (0, width - line.shape[1]))),
        ]
    )
    arrivals = {0: own}
    for group in GROUPS[1:]:
        for offset in group:
            toward = 1 if offset < 0 else -1
            arrivals[offset] = hop(arrivals[offset + toward], toward)
    everyone = [arrivals[offset] for group in GROUPS for offset in group]

    preacts = jnp.concatenate([saved_preacts[0, 0, 0], saved_preacts[0, 1, 0]], axis=1)
    preacts = preacts.reshape(columns, DEPTH, span, -1)
    received, sides, hidden, parts = [], [], [], []
    for n, group in enumerate(GROUPS):
        last = group == GROUPS[-1]
        earlier = sides[n - 2 : n - 1] if n >= 2 else [preacts] * n
        sent = pack(
            place(group),
            [arrivals[offset] for offset in group],
            columns,
            capacity,
            everyone if last else (),
            earlier,
        )
        got = exchange(sent)
        received.append(got)
        if not last:
            pieces = prepare(place(group), got, preacts, down_proj)
            sides.append(pieces[0])
            hidden.append(pieces[1])
            parts.append(pieces[2])
    last = received[-1]
    final_hidden, sending = turn(place(GROUPS[-1]), last, preacts, down_proj, gate_up, parts)
    hidden.append(final_hidden)

    first = [sum(len(group) for group in GROUPS[:n]) for n in range(len(GROUPS))]
    part_rows = None
    coming = []
    folded = []
    down_grad = None
    for n in reversed(range(len(GROUPS))):
        group = GROUPS[n]
        returned = exchange(sending)
        if part_rows is None:
            part_rows = returned
        earlier = []
        if n > 0:
            if n == len(GROUPS) - 3:
                down_grad = down_grads(received, hidden, width)
                folded = list(folded) + [down_grad]
            sending = slice_grad(first[n - 1], sides[n - 1], last, gate_up, folded)
            earlier = [sending]
        folded = fold(
            place(group),
            first[n],
            part_rows,
            returned,
            [arrivals[offset] for offset in group],
            coming,
            capacity,
            n == 0,
            earlier,
        )
        if n > 0:
            coming = [hop(block, -1 if offset < 0 else 1) for block, offset in zip(folded, group)]
    above, below, probs = folded
    prob_grad = jnp.moveaxis(probs[0].reshape(2, 2, tokens), 0, 2)
    return (shifted(above, -1)[None], shifted(below, 1)[None], prob_grad[None], down_grad[None, None])


def solution(mesh):
    sections, slices = mesh.devices.shape
    grid = Mesh(mesh.devices.reshape(sections, slices // DEPTH, DEPTH), ("section", "column", "depth"))
    spread = ("column", "depth")
    in_specs = (
        P("section", None, spread, None),
        P("section", None, spread, None),
        P("section", None, spread, None),
        P("section", None, spread, None, None, None),
        P("section", spread, None, None),
        P("section", spread, None, None),
    )
    out_specs = (
        P("section", spread, None),
        P("section", spread, None),
        P("section", None, spread, None),
        P("section", spread, None, None),
    )
    return jax.shard_map(shards, mesh=grid, in_specs=in_specs, out_specs=out_specs, check_vma=False)
```

```python
import functools

import jax
import jax.numpy as jnp
from jax import lax
from jax.experimental import pallas as pl
from jax.experimental.pallas import tpu as pltpu
from jax.sharding import Mesh, PartitionSpec as P

SHARE = 4
DEPTH = 2 * SHARE
GROUPS = ((0,), (-1, 1), (-2, 2), (-3, 3), (-4,))
EXTRA = 128
HALF = 64
LANES = 128
META = 8
TILE = 512
VMEM_LIMIT = 63 * 1024 * 1024

f32 = jnp.float32
bf16 = jnp.bfloat16
NT = (((1,), (1,)), ((), ()))
TN = (((0,), (0,)), ((), ()))


def tags(rows):
    meta = rows[LANES : LANES + META, : 4 * LANES].astype(f32)
    return [meta[0:1, k * LANES : (k + 1) * LANES] for k in range(4)]


def slot_hits(picks, half, count, capacity):
    ids = (half + 2 * lax.broadcasted_iota(jnp.int32, (count, LANES), 0)).astype(f32)
    named = (picks[0] == ids) | (picks[1] == ids)
    row = lax.broadcasted_iota(jnp.int32, (LANES, LANES), 0)
    col = lax.broadcasted_iota(jnp.int32, (LANES, LANES), 1)
    earlier = (row < col) & (row // HALF == col // HALF)
    before = jnp.dot(
        named.astype(f32).astype(bf16), earlier.astype(f32).astype(bf16), preferred_element_type=f32
    )
    stretch = lax.broadcasted_iota(jnp.int32, (count, LANES), 1) // HALF
    keys = jnp.where(named, before + (stretch * capacity).astype(f32), -1.0)
    slot = lax.broadcasted_iota(jnp.int32, (count, 2 * capacity, LANES), 1).astype(f32)
    return jnp.where(slot == keys[:, None, :], 1.0, 0.0), ids


def flat(hits):
    return hits.reshape(-1, LANES).astype(bf16)


def tiles(width):
    return [slice(low, low + TILE) for low in range(0, width, TILE)]


def params():
    return pltpu.CompilerParams(vmem_limit_bytes=VMEM_LIMIT)


SMEM = pl.BlockSpec(memory_space=pltpu.SMEM)
VMEM = pl.BlockSpec(memory_space=pltpu.VMEM)
ANY = pl.BlockSpec(memory_space=pl.ANY)


def pack_kernel(capacity, count, tagged, width, place, *refs):
    out = refs[-1]
    columns = out.shape[0]
    for m in range(count):
        rows = refs[m]
        hits, _ = slot_hits(tags(rows), place[0], columns, capacity)
        ones = flat(hits)
        for tile in tiles(width):
            packed = jnp.dot(ones, rows[:LANES, tile], preferred_element_type=f32)
            out[:, m, :, tile] = packed.astype(bf16).reshape(columns, 2 * capacity, TILE)
    if out.shape[3] > width:
        lane = lax.broadcasted_iota(jnp.int32, (columns, 2 * capacity, EXTRA), 2)
        scales = jnp.zeros((columns, 2 * capacity, EXTRA), f32)
        for k, rows in enumerate(refs[count : count + tagged]):
            meta = rows[:, :].astype(f32)
            picks = [meta[0:1, i * LANES : (i + 1) * LANES] for i in range(4)]
            hits, ids = slot_hits(picks, place[0], columns, capacity)
            gates = jnp.where(picks[0] == ids, picks[2], 0.0) + jnp.where(picks[1] == ids, picks[3], 0.0)
            scale = jnp.sum(hits * gates[:, None, :], axis=2, keepdims=True)
            scales = jnp.where(lane == k, scale, scales)
        out[:, 0, :, width:] = scales.astype(bf16)


def pack(place, arrivals, columns, capacity, tagged=(), earlier=()):
    width = arrivals[0].shape[1]
    extra = EXTRA if tagged else 0
    only_tags = pl.BlockSpec((META, 4 * LANES), lambda i: (LANES // META, 0))
    return pl.pallas_call(
        functools.partial(pack_kernel, capacity, len(arrivals), len(tagged), width),
        out_shape=jax.ShapeDtypeStruct((columns, len(arrivals), 2 * capacity, width + extra), bf16),
        grid=(1,),
        in_specs=[SMEM] + [VMEM] * len(arrivals) + [only_tags] * len(tagged) + [ANY] * len(earlier),
        out_specs=VMEM,
        compiler_params=params(),
        name="pack_rows",
    )(place, *arrivals, *tagged, *earlier)


def expert_parts(rows, preacts, down_proj):
    width = down_proj.shape[1]
    half = down_proj.shape[0]
    back = lax.dot_general(rows, down_proj, NT, preferred_element_type=f32)
    gate_pre = preacts[:, :half].astype(f32)
    up_pre = preacts[:, half:].astype(f32)
    sig = 1.0 / (1.0 + jnp.exp(-gate_pre))
    act = gate_pre * sig
    hidden = act * up_pre
    part = jnp.sum(hidden * back, axis=1, keepdims=True)
    gate_side = back * up_pre * sig * (1.0 + gate_pre * (1.0 - sig))
    return gate_side, back * act, hidden, part


def prepare_kernel(width, place, rows, preacts, down_proj, sides, hidden, parts):
    slots = sides.shape[1]
    half = hidden.shape[2]
    table = rows[:, 0, :, :width].reshape(slots, width)
    pre = preacts[:, 0].reshape(slots, 2 * half)
    gate_side, up_side, hid, part = expert_parts(table, pre, down_proj[...])
    sides[0, :, :half] = gate_side
    sides[0, :, half:] = up_side
    hidden[0] = hid
    parts[0] = jnp.broadcast_to(part, (slots, EXTRA))


def prepare(place, received, preacts, down_proj):
    columns, count, span = received.shape[:3]
    half, width = down_proj.shape
    slots = columns * span
    block = lambda m, place: (m, 0, 0)
    return pl.pallas_call(
        functools.partial(prepare_kernel, width),
        out_shape=[
            jax.ShapeDtypeStruct((count, slots, 2 * half), f32),
            jax.ShapeDtypeStruct((count, slots, half), f32),
            jax.ShapeDtypeStruct((count, slots, EXTRA), f32),
        ],
        grid_spec=pltpu.PrefetchScalarGridSpec(
            num_scalar_prefetch=1,
            grid=(count,),
            in_specs=[
                pl.BlockSpec((columns, 1, span, width), lambda m, place: (0, m, 0, 0)),
                pl.BlockSpec((columns, 1, span, 2 * half), lambda m, place: (0, place[1 + m], 0, 0)),
                pl.BlockSpec((half, width), lambda m, place: (0, 0)),
            ],
            out_specs=[
                pl.BlockSpec((1, slots, 2 * half), block),
                pl.BlockSpec((1, slots, half), block),
                pl.BlockSpec((1, slots, EXTRA), block),
            ],
        ),
        compiler_params=params(),
        name="prepare",
    )(place, received, preacts, down_proj)


def turn_kernel(count, place, received, preacts, down_proj, gate_up, *refs):
    others, hidden, out = refs[:-2], refs[-2], refs[-1]
    half, width = down_proj.shape
    columns, _, span, _ = received.shape
    slots = columns * span
    table = received[:, 0, :, :width].reshape(slots, width)
    scales = received[:, 0, :, width:].astype(f32).reshape(slots, EXTRA)
    gate_side, up_side, hid, part = expert_parts(table, preacts[:, 0].reshape(slots, 2 * half), down_proj[...])
    hidden[0] = hid
    scale = scales[:, count - 1 : count]
    both = jnp.concatenate([scale * gate_side, scale * up_side], axis=1).astype(bf16)
    for tile in tiles(width):
        grad = lax.dot_general(both, gate_up[tile, :], NT, preferred_element_type=f32)
        out[:, 0, :, tile] = grad.astype(bf16).reshape(columns, span, TILE)
    lane = lax.broadcasted_iota(jnp.int32, (slots, EXTRA), 1)
    parts = jnp.where(lane == count - 1, part, 0.0)
    k = 0
    for group in others:
        for m in range(group.shape[0]):
            parts = jnp.where(lane == k, group[m], parts)
            k += 1
    out[:, 0, :, width:] = parts.astype(bf16).reshape(columns, span, EXTRA)


def turn(place, received, preacts, down_proj, gate_up, parts):
    columns, _, span, wide = received.shape
    half, width = down_proj.shape
    slots = columns * span
    count = 1 + sum(p.shape[0] for p in parts)
    return pl.pallas_call(
        functools.partial(turn_kernel, count),
        out_shape=[
            jax.ShapeDtypeStruct((1, slots, half), f32),
            jax.ShapeDtypeStruct((columns, 1, span, wide), bf16),
        ],
        grid_spec=pltpu.PrefetchScalarGridSpec(
            num_scalar_prefetch=1,
            grid=(1,),
            in_specs=[
                VMEM,
                pl.BlockSpec((columns, 1, span, 2 * half), lambda m, place: (0, place[1], 0, 0)),
                VMEM,
                VMEM,
            ]
            + [VMEM] * len(parts),
            out_specs=[VMEM, VMEM],
        ),
        compiler_params=params(),
        name="turn",
    )(place, received, preacts, down_proj, gate_up, *parts)


def grad_kernel(first, sides, last, gate_up, *rest):
    out = rest[-1]
    width = gate_up.shape[0]
    columns, _, span, _ = out.shape
    slots = columns * span
    scales = last[:, 0].reshape(slots, EXTRA).astype(f32)
    lane = lax.broadcasted_iota(jnp.int32, (slots, EXTRA), 1)
    index = first + pl.program_id(0)
    scale = jnp.sum(jnp.where(lane == index, scales, 0.0), axis=1, keepdims=True)
    both = (scale * sides[0]).astype(bf16)
    for tile in tiles(width):
        grad = lax.dot_general(both, gate_up[tile, :], NT, preferred_element_type=f32)
        out[:, 0, :, tile] = grad.astype(bf16).reshape(columns, span, TILE)


def slice_grad(first, sides, last, gate_up, earlier):
    count, slots, full = sides.shape
    columns, _, span, wide = last.shape
    width = gate_up.shape[0]
    return pl.pallas_call(
        functools.partial(grad_kernel, first),
        out_shape=jax.ShapeDtypeStruct((columns, count, span, width), bf16),
        grid=(count,),
        in_specs=[
            pl.BlockSpec((1, slots, full), lambda m: (m, 0, 0)),
            pl.BlockSpec((columns, 1, span, EXTRA), lambda m: (0, 0, 0, width // EXTRA)),
            pl.BlockSpec((width, full), lambda m: (0, 0)),
        ]
        + [ANY] * len(earlier),
        out_specs=pl.BlockSpec((columns, 1, span, width), lambda m: (0, m, 0, 0)),
        compiler_params=params(),
        name="slice_grad",
    )(sides, last, gate_up, *earlier)


def down_kernel(groups, last, *refs):
    rows, hidden, out, scaled = refs[:groups], refs[groups : 2 * groups], refs[-2], refs[-1]
    slots = hidden[0].shape[1]

    @pl.when(pl.program_id(0) == 0)
    def _():
        scales = last[:, 0].reshape(slots, EXTRA).astype(f32)
        k = 0
        for group in hidden:
            for m in range(group.shape[0]):
                scaled[k * slots : (k + 1) * slots] = (scales[:, k : k + 1] * group[m]).astype(bf16)
                k += 1

    total = jnp.zeros(out.shape, f32)
    k = 0
    for group in rows:
        for m in range(group.shape[1]):
            table = group[:, m].reshape(slots, out.shape[1])
            part = scaled[k * slots : (k + 1) * slots]
            total += lax.dot_general(part, table, TN, preferred_element_type=f32)
            k += 1
    out[...] = total.astype(bf16)


def down_grads(received, hidden, width):
    last = received[-1]
    columns, _, span, _ = last.shape
    count = sum(h.shape[0] for h in hidden)
    slots, half = hidden[0].shape[1:]
    return pl.pallas_call(
        functools.partial(down_kernel, len(received)),
        out_shape=jax.ShapeDtypeStruct((half, width), bf16),
        grid=(width // TILE,),
        in_specs=[pl.BlockSpec((columns, 1, span, EXTRA), lambda i: (0, 0, 0, width // EXTRA))]
        + [pl.BlockSpec((columns, g.shape[1], span, TILE), lambda i: (0, 0, 0, i)) for g in received]
        + [pl.BlockSpec(h.shape, lambda i: (0, 0, 0)) for h in hidden],
        out_specs=pl.BlockSpec((half, TILE), lambda i: (0, i)),
        scratch_shapes=[pltpu.VMEM((count * slots, half), bf16)],
        compiler_params=params(),
        name="down_grads",
    )(last, *received, *hidden)


def fold_kernel(capacity, first, count, coming, final, place, parts, *refs):
    returned = refs[0]
    metas = refs[1 : 1 + count]
    incoming = refs[1 + count : 1 + count + coming]
    outs = refs[-3:] if final else refs[-count:]
    columns, _, span, _ = returned.shape
    slots = columns * span
    table = parts[:, 0].astype(f32)
    for m in range(count):
        meta = metas[m][:, :].astype(f32)
        picks = [meta[0:1, i * LANES : (i + 1) * LANES] for i in range(4)]
        hits, ids = slot_hits(picks, place[0], columns, capacity)
        ones = flat(hits)
        added = list(incoming) if final else list(incoming[m : m + 1])
        for tile in tiles(returned.shape[3] // TILE * TILE):
            rows = returned[:, m, :, tile].reshape(slots, TILE)
            total = lax.dot_general(ones, rows, TN, preferred_element_type=f32)
            for other in added:
                total = total + other[:LANES, tile].astype(f32)
            total = total.astype(bf16)
            if final:
                outs[0][:, tile] = total[:HALF]
                outs[1][:, tile] = total[HALF:]
            else:
                outs[m][:LANES, tile] = total
        values = hits * table[:, :, first + m : first + m + 1]
        for k in range(2):
            named = jnp.where(picks[k] == ids, 1.0, 0.0)[:, None, :]
            line = jnp.sum(jnp.sum(values * named, axis=1), axis=0, keepdims=True)
            lanes = slice(k * LANES, (k + 1) * LANES)
            for other in added:
                line = line + other[LANES : LANES + META, lanes].astype(f32)[0:1]
            if final:
                outs[2][:, lanes] = jnp.broadcast_to(line, (META, LANES))
            else:
                outs[m][LANES : LANES + META, lanes] = jnp.broadcast_to(line, (META, LANES)).astype(bf16)


def fold(place, first, parts, returned, arrivals, incoming, capacity, final, earlier=()):
    columns, count, span, _ = returned.shape
    width = arrivals[0].shape[1]
    only_tags = pl.BlockSpec((META, 4 * LANES), lambda i: (LANES // META, 0))
    if final:
        shapes = [jax.ShapeDtypeStruct((HALF, width), bf16)] * 2
        shapes.append(jax.ShapeDtypeStruct((META, 2 * LANES), f32))
    else:
        shapes = [jax.ShapeDtypeStruct((LANES + META, width), bf16)] * count
    return pl.pallas_call(
        functools.partial(fold_kernel, capacity, first, count, len(incoming), final),
        out_shape=shapes,
        grid=(1,),
        in_specs=[SMEM, pl.BlockSpec((columns, 1, span, EXTRA), lambda i: (0, 0, 0, width // EXTRA)), VMEM]
        + [only_tags] * count
        + [VMEM] * len(incoming)
        + [ANY] * len(earlier),
        out_specs=[VMEM] * len(shapes),
        compiler_params=params(),
        name="fold_rows",
    )(place, parts, returned, *arrivals, *incoming, *earlier)


def exchange(block):
    return lax.all_to_all(block, "column", split_axis=0, concat_axis=0, tiled=True)


def hop(block, distance):
    return lax.ppermute(block, "depth", [(i, (i + distance) % DEPTH) for i in range(DEPTH)])


def shifted(block, distance):
    devices = range(lax.axis_size("section"))
    route = [(i - distance, i) for i in devices if i - distance in devices]
    return lax.ppermute(block, "section", route)


def shards(grad_out, gate_probs, routes, saved_preacts, w_gate_up, w_down):
    columns = lax.axis_size("column")
    capacity = saved_preacts.shape[4]
    span = 2 * capacity
    width = grad_out.shape[3]
    tokens = grad_out.shape[2]
    level = lax.axis_index("depth")
    half = level // SHARE
    gate_up = w_gate_up[0, 0]
    down_proj = w_down[0, 0]

    def place(group):
        where = [half] + [(level + DEPTH + offset) % DEPTH for offset in group]
        return jnp.stack(where).astype(jnp.int32)

    picks = jnp.moveaxis(routes[0], 2, 0).reshape(1, 4 * tokens).astype(bf16)
    gates = jnp.moveaxis(gate_probs[0], 2, 0).reshape(1, 4 * tokens)
    line = jnp.concatenate([picks, gates], axis=1)
    own = jnp.concatenate(
        [
            grad_out[0].reshape(2 * tokens, width),
            jnp.pad(line, ((0, META - 1), (0, width - line.shape[1]))),
        ]
    )
    arrivals = {0: own}
    for group in GROUPS[1:]:
        for offset in group:
            toward = 1 if offset < 0 else -1
            arrivals[offset] = hop(arrivals[offset + toward], toward)
    everyone = [arrivals[offset] for group in GROUPS for offset in group]

    preacts = jnp.concatenate([saved_preacts[0, 0, 0], saved_preacts[0, 1, 0]], axis=1)
    preacts = preacts.reshape(columns, DEPTH, span, -1)
    received, sides, hidden, parts = [], [], [], []
    for n, group in enumerate(GROUPS):
        last = group == GROUPS[-1]
        earlier = sides[n - 2 : n - 1] if n >= 2 else [preacts] * n
        sent = pack(
            place(group),
            [arrivals[offset] for offset in group],
            columns,
            capacity,
            everyone if last else (),
            earlier,
        )
        got = exchange(sent)
        received.append(got)
        if not last:
            pieces = prepare(place(group), got, preacts, down_proj)
            sides.append(pieces[0])
            hidden.append(pieces[1])
            parts.append(pieces[2])
    last = received[-1]
    final_hidden, sending = turn(place(GROUPS[-1]), last, preacts, down_proj, gate_up, parts)
    hidden.append(final_hidden)

    first = [sum(len(group) for group in GROUPS[:n]) for n in range(len(GROUPS))]
    part_rows = None
    coming = []
    folded = []
    down_grad = None
    for n in reversed(range(len(GROUPS))):
        group = GROUPS[n]
        returned = exchange(sending)
        if part_rows is None:
            part_rows = returned
        earlier = []
        if n > 0:
            held = list(coming)
            if n == len(GROUPS) - 3:
                down_grad = down_grads(received, hidden, width)
                held.append(down_grad)
            sending = slice_grad(first[n - 1], sides[n - 1], last, gate_up, held)
            earlier = [sending]
        folded = fold(
            place(group),
            first[n],
            part_rows,
            returned,
            [arrivals[offset] for offset in group],
            coming,
            capacity,
            n == 0,
            earlier,
        )
        if n > 0:
            coming = [hop(block, -1 if offset < 0 else 1) for block, offset in zip(folded, group)]
    above, below, probs = folded
    prob_grad = jnp.moveaxis(probs[0].reshape(2, 2, tokens), 0, 2)
    return (shifted(above, -1)[None], shifted(below, 1)[None], prob_grad[None], down_grad[None, None])


def solution(mesh):
    sections, slices = mesh.devices.shape
    grid = Mesh(mesh.devices.reshape(sections, slices // DEPTH, DEPTH), ("section", "column", "depth"))
    spread = ("column", "depth")
    in_specs = (
        P("section", None, spread, None),
        P("section", None, spread, None),
        P("section", None, spread, None),
        P("section", None, spread, None, None, None),
        P("section", spread, None, None),
        P("section", spread, None, None),
    )
    out_specs = (
        P("section", spread, None),
        P("section", spread, None),
        P("section", None, spread, None),
        P("section", spread, None, None),
    )
    return jax.shard_map(shards, mesh=grid, in_specs=in_specs, out_specs=out_specs, check_vma=False)
```

```python
import functools

import jax
import jax.numpy as jnp
from jax import lax
from jax.experimental import pallas as pl
from jax.experimental.pallas import tpu as pltpu
from jax.sharding import Mesh, PartitionSpec as P

SHARE = 4
DEPTH = 2 * SHARE
GROUPS = ((0,), (-1, 1), (-2, 2), (-3, 3), (-4,))
EXTRA = 128
HALF = 64
LANES = 128
META = 8
TILE = 512
VMEM_LIMIT = 63 * 1024 * 1024

f32 = jnp.float32
bf16 = jnp.bfloat16
NT = (((1,), (1,)), ((), ()))
TN = (((0,), (0,)), ((), ()))


def tags(rows):
    meta = rows[LANES : LANES + META, : 4 * LANES].astype(f32)
    return [meta[0:1, k * LANES : (k + 1) * LANES] for k in range(4)]


def slot_hits(picks, half, count, capacity):
    ids = (half + 2 * lax.broadcasted_iota(jnp.int32, (count, LANES), 0)).astype(f32)
    named = (picks[0] == ids) | (picks[1] == ids)
    row = lax.broadcasted_iota(jnp.int32, (LANES, LANES), 0)
    col = lax.broadcasted_iota(jnp.int32, (LANES, LANES), 1)
    earlier = (row < col) & (row // HALF == col // HALF)
    before = jnp.dot(
        named.astype(f32).astype(bf16), earlier.astype(f32).astype(bf16), preferred_element_type=f32
    )
    stretch = lax.broadcasted_iota(jnp.int32, (count, LANES), 1) // HALF
    keys = jnp.where(named, before + (stretch * capacity).astype(f32), -1.0)
    slot = lax.broadcasted_iota(jnp.int32, (count, 2 * capacity, LANES), 1).astype(f32)
    return jnp.where(slot == keys[:, None, :], 1.0, 0.0), ids


def flat(hits):
    return hits.reshape(-1, LANES).astype(bf16)


def tiles(width):
    return [slice(low, low + TILE) for low in range(0, width, TILE)]


def params():
    return pltpu.CompilerParams(vmem_limit_bytes=VMEM_LIMIT)


SMEM = pl.BlockSpec(memory_space=pltpu.SMEM)
VMEM = pl.BlockSpec(memory_space=pltpu.VMEM)
ANY = pl.BlockSpec(memory_space=pl.ANY)


def pack_kernel(capacity, count, tagged, width, place, *refs):
    out = refs[-1]
    columns = out.shape[0]
    for m in range(count):
        rows = refs[m]
        hits, _ = slot_hits(tags(rows), place[0], columns, capacity)
        ones = flat(hits)
        for tile in tiles(width):
            packed = jnp.dot(ones, rows[:LANES, tile], preferred_element_type=f32)
            out[:, m, :, tile] = packed.astype(bf16).reshape(columns, 2 * capacity, TILE)
    if out.shape[3] > width:
        lane = lax.broadcasted_iota(jnp.int32, (columns, 2 * capacity, EXTRA), 2)
        scales = jnp.zeros((columns, 2 * capacity, EXTRA), f32)
        for k, rows in enumerate(refs[count : count + tagged]):
            meta = rows[:, :].astype(f32)
            picks = [meta[0:1, i * LANES : (i + 1) * LANES] for i in range(4)]
            hits, ids = slot_hits(picks, place[0], columns, capacity)
            gates = jnp.where(picks[0] == ids, picks[2], 0.0) + jnp.where(picks[1] == ids, picks[3], 0.0)
            scale = jnp.sum(hits * gates[:, None, :], axis=2, keepdims=True)
            scales = jnp.where(lane == k, scale, scales)
        out[:, 0, :, width:] = scales.astype(bf16)


def pack(place, arrivals, columns, capacity, tagged=(), earlier=()):
    width = arrivals[0].shape[1]
    extra = EXTRA if tagged else 0
    only_tags = pl.BlockSpec((META, 4 * LANES), lambda i: (LANES // META, 0))
    return pl.pallas_call(
        functools.partial(pack_kernel, capacity, len(arrivals), len(tagged), width),
        out_shape=jax.ShapeDtypeStruct((columns, len(arrivals), 2 * capacity, width + extra), bf16),
        grid=(1,),
        in_specs=[SMEM] + [VMEM] * len(arrivals) + [only_tags] * len(tagged) + [ANY] * len(earlier),
        out_specs=VMEM,
        compiler_params=params(),
        name="pack_rows",
    )(place, *arrivals, *tagged, *earlier)


def expert_parts(rows, preacts, down_proj):
    width = down_proj.shape[1]
    half = down_proj.shape[0]
    back = lax.dot_general(rows, down_proj, NT, preferred_element_type=f32)
    gate_pre = preacts[:, :half].astype(f32)
    up_pre = preacts[:, half:].astype(f32)
    sig = 1.0 / (1.0 + jnp.exp(-gate_pre))
    act = gate_pre * sig
    hidden = act * up_pre
    part = jnp.sum(hidden * back, axis=1, keepdims=True)
    gate_side = back * up_pre * sig * (1.0 + gate_pre * (1.0 - sig))
    return gate_side, back * act, hidden, part


def prepare_kernel(width, place, rows, preacts, down_proj, sides, hidden, parts):
    slots = sides.shape[1]
    half = hidden.shape[2]
    table = rows[:, 0, :, :width].reshape(slots, width)
    pre = preacts[:, 0].reshape(slots, 2 * half)
    gate_side, up_side, hid, part = expert_parts(table, pre, down_proj[...])
    sides[0, :, :half] = gate_side
    sides[0, :, half:] = up_side
    hidden[0] = hid
    parts[0] = jnp.broadcast_to(part, (slots, EXTRA))


def prepare(place, received, preacts, down_proj):
    columns, count, span = received.shape[:3]
    half, width = down_proj.shape
    slots = columns * span
    block = lambda m, place: (m, 0, 0)
    return pl.pallas_call(
        functools.partial(prepare_kernel, width),
        out_shape=[
            jax.ShapeDtypeStruct((count, slots, 2 * half), f32),
            jax.ShapeDtypeStruct((count, slots, half), f32),
            jax.ShapeDtypeStruct((count, slots, EXTRA), f32),
        ],
        grid_spec=pltpu.PrefetchScalarGridSpec(
            num_scalar_prefetch=1,
            grid=(count,),
            in_specs=[
                pl.BlockSpec((columns, 1, span, width), lambda m, place: (0, m, 0, 0)),
                pl.BlockSpec((columns, 1, span, 2 * half), lambda m, place: (0, place[1 + m], 0, 0)),
                pl.BlockSpec((half, width), lambda m, place: (0, 0)),
            ],
            out_specs=[
                pl.BlockSpec((1, slots, 2 * half), block),
                pl.BlockSpec((1, slots, half), block),
                pl.BlockSpec((1, slots, EXTRA), block),
            ],
        ),
        compiler_params=params(),
        name="prepare",
    )(place, received, preacts, down_proj)


def turn_kernel(count, place, received, preacts, down_proj, gate_up, *refs):
    others, hidden, out = refs[:-2], refs[-2], refs[-1]
    half, width = down_proj.shape
    columns, _, span, _ = received.shape
    slots = columns * span
    table = received[:, 0, :, :width].reshape(slots, width)
    scales = received[:, 0, :, width:].astype(f32).reshape(slots, EXTRA)
    gate_side, up_side, hid, part = expert_parts(table, preacts[:, 0].reshape(slots, 2 * half), down_proj[...])
    hidden[0] = hid
    scale = scales[:, count - 1 : count]
    both = jnp.concatenate([scale * gate_side, scale * up_side], axis=1).astype(bf16)
    for tile in tiles(width):
        grad = lax.dot_general(both, gate_up[tile, :], NT, preferred_element_type=f32)
        out[:, 0, :, tile] = grad.astype(bf16).reshape(columns, span, TILE)
    lane = lax.broadcasted_iota(jnp.int32, (slots, EXTRA), 1)
    parts = jnp.where(lane == count - 1, part, 0.0)
    k = 0
    for group in others:
        for m in range(group.shape[0]):
            parts = jnp.where(lane == k, group[m], parts)
            k += 1
    out[:, 0, :, width:] = parts.astype(bf16).reshape(columns, span, EXTRA)


def turn(place, received, preacts, down_proj, gate_up, parts):
    columns, _, span, wide = received.shape
    half, width = down_proj.shape
    slots = columns * span
    count = 1 + sum(p.shape[0] for p in parts)
    return pl.pallas_call(
        functools.partial(turn_kernel, count),
        out_shape=[
            jax.ShapeDtypeStruct((1, slots, half), f32),
            jax.ShapeDtypeStruct((columns, 1, span, wide), bf16),
        ],
        grid_spec=pltpu.PrefetchScalarGridSpec(
            num_scalar_prefetch=1,
            grid=(1,),
            in_specs=[
                VMEM,
                pl.BlockSpec((columns, 1, span, 2 * half), lambda m, place: (0, place[1], 0, 0)),
                VMEM,
                VMEM,
            ]
            + [VMEM] * len(parts),
            out_specs=[VMEM, VMEM],
        ),
        compiler_params=params(),
        name="turn",
    )(place, received, preacts, down_proj, gate_up, *parts)


def grad_kernel(first, sides, last, gate_up, *rest):
    out = rest[-1]
    width = gate_up.shape[0]
    columns, _, span, _ = out.shape
    slots = columns * span
    scales = last[:, 0].reshape(slots, EXTRA).astype(f32)
    lane = lax.broadcasted_iota(jnp.int32, (slots, EXTRA), 1)
    index = first + pl.program_id(0)
    scale = jnp.sum(jnp.where(lane == index, scales, 0.0), axis=1, keepdims=True)
    both = (scale * sides[0]).astype(bf16)
    for tile in tiles(width):
        grad = lax.dot_general(both, gate_up[tile, :], NT, preferred_element_type=f32)
        out[:, 0, :, tile] = grad.astype(bf16).reshape(columns, span, TILE)


def slice_grad(first, sides, last, gate_up, earlier):
    count, slots, full = sides.shape
    columns, _, span, _ = last.shape
    width = gate_up.shape[0]
    shape = jax.ShapeDtypeStruct((columns, count, span, width), bf16)
    most = width - TILE
    shared = [
        pl.BlockSpec((1, slots, full), lambda m: (m, 0, 0)),
        pl.BlockSpec((columns, 1, span, EXTRA), lambda m: (0, 0, 0, width // EXTRA)),
    ]
    sending = pl.pallas_call(
        functools.partial(grad_kernel, first),
        out_shape=shape,
        grid=(count,),
        in_specs=shared + [pl.BlockSpec((most, full), lambda m: (0, 0))],
        out_specs=pl.BlockSpec((columns, 1, span, most), lambda m: (0, m, 0, 0)),
        compiler_params=params(),
        name="slice_grad",
    )(sides, last, gate_up)
    return pl.pallas_call(
        functools.partial(grad_kernel, first),
        out_shape=shape,
        grid=(count,),
        in_specs=shared
        + [pl.BlockSpec((TILE, full), lambda m: (most // TILE, 0)), ANY]
        + [ANY] * len(earlier),
        out_specs=pl.BlockSpec((columns, 1, span, TILE), lambda m: (0, m, 0, most // TILE)),
        input_output_aliases={3: 0},
        compiler_params=params(),
        name="slice_grad_end",
    )(sides, last, gate_up, sending, *earlier)


def down_kernel(groups, last, *refs):
    rows, hidden, out, scaled = refs[:groups], refs[groups : 2 * groups], refs[-2], refs[-1]
    slots = hidden[0].shape[1]

    @pl.when(pl.program_id(0) == 0)
    def _():
        scales = last[:, 0].reshape(slots, EXTRA).astype(f32)
        k = 0
        for group in hidden:
            for m in range(group.shape[0]):
                scaled[k * slots : (k + 1) * slots] = (scales[:, k : k + 1] * group[m]).astype(bf16)
                k += 1

    total = jnp.zeros(out.shape, f32)
    k = 0
    for group in rows:
        for m in range(group.shape[1]):
            table = group[:, m].reshape(slots, out.shape[1])
            part = scaled[k * slots : (k + 1) * slots]
            total += lax.dot_general(part, table, TN, preferred_element_type=f32)
            k += 1
    out[...] = total.astype(bf16)


def down_grads(received, hidden, width):
    last = received[-1]
    columns, _, span, _ = last.shape
    count = sum(h.shape[0] for h in hidden)
    slots, half = hidden[0].shape[1:]
    return pl.pallas_call(
        functools.partial(down_kernel, len(received)),
        out_shape=jax.ShapeDtypeStruct((half, width), bf16),
        grid=(width // TILE,),
        in_specs=[pl.BlockSpec((columns, 1, span, EXTRA), lambda i: (0, 0, 0, width // EXTRA))]
        + [pl.BlockSpec((columns, g.shape[1], span, TILE), lambda i: (0, 0, 0, i)) for g in received]
        + [pl.BlockSpec(h.shape, lambda i: (0, 0, 0)) for h in hidden],
        out_specs=pl.BlockSpec((half, TILE), lambda i: (0, i)),
        scratch_shapes=[pltpu.VMEM((count * slots, half), bf16)],
        compiler_params=params(),
        name="down_grads",
    )(last, *received, *hidden)


def fold_kernel(capacity, first, count, coming, split, place, parts, *refs):
    returned = refs[0]
    metas = refs[1 : 1 + count]
    incoming = refs[1 + count : 1 + count + coming]
    outs = refs[-3 * count :] if split else refs[-count:]
    columns, _, span, _ = returned.shape
    slots = columns * span
    table = parts[:, 0].astype(f32)
    for m in range(count):
        meta = metas[m][:, :].astype(f32)
        picks = [meta[0:1, i * LANES : (i + 1) * LANES] for i in range(4)]
        hits, ids = slot_hits(picks, place[0], columns, capacity)
        ones = flat(hits)
        added = incoming[m::count] if coming >= count else incoming[m : m + 1]
        sums = [other for other in added if other.shape[0] > META]
        for tile in tiles(returned.shape[3] // TILE * TILE):
            rows = returned[:, m, :, tile].reshape(slots, TILE)
            total = lax.dot_general(ones, rows, TN, preferred_element_type=f32)
            for other in sums:
                total = total + other[:LANES, tile].astype(f32)
            total = total.astype(bf16)
            if split:
                outs[3 * m][:, tile] = total[:HALF]
                outs[3 * m + 1][:, tile] = total[HALF:]
            else:
                outs[m][:LANES, tile] = total
        values = hits * table[:, :, first + m : first + m + 1]
        for k in range(2):
            named = jnp.where(picks[k] == ids, 1.0, 0.0)[:, None, :]
            line = jnp.sum(jnp.sum(values * named, axis=1), axis=0, keepdims=True)
            lanes = slice(k * LANES, (k + 1) * LANES)
            for other in added:
                low = LANES if other.shape[0] > META else 0
                line = line + other[low : low + META, lanes].astype(f32)[0:1]
            line = jnp.broadcast_to(line, (META, LANES)).astype(bf16)
            if split:
                outs[3 * m + 2][:, lanes] = line
            else:
                outs[m][LANES : LANES + META, lanes] = line


def fold(place, first, parts, returned, arrivals, incoming, capacity, split, earlier=()):
    columns, count, span, _ = returned.shape
    width = arrivals[0].shape[1]
    only_tags = pl.BlockSpec((META, 4 * LANES), lambda i: (LANES // META, 0))
    if split:
        halves = [jax.ShapeDtypeStruct((HALF, width), bf16)] * 2
        shapes = (halves + [jax.ShapeDtypeStruct((META, 2 * LANES), bf16)]) * count
    else:
        shapes = [jax.ShapeDtypeStruct((LANES + META, width), bf16)] * count
    return pl.pallas_call(
        functools.partial(fold_kernel, capacity, first, count, len(incoming), split),
        out_shape=shapes,
        grid=(1,),
        in_specs=[SMEM, pl.BlockSpec((columns, 1, span, EXTRA), lambda i: (0, 0, 0, width // EXTRA)), VMEM]
        + [only_tags] * count
        + [VMEM] * len(incoming)
        + [ANY] * len(earlier),
        out_specs=[VMEM] * len(shapes),
        compiler_params=params(),
        name="fold_rows",
    )(place, parts, returned, *arrivals, *incoming, *earlier)


def exchange(block):
    return lax.all_to_all(block, "column", split_axis=0, concat_axis=0, tiled=True)


def hop(block, distance):
    return lax.ppermute(block, "depth", [(i, (i + distance) % DEPTH) for i in range(DEPTH)])


def shifted(block, distance, along=0):
    sections = lax.axis_size("section")
    route = [
        (i * DEPTH + z, (i + distance) * DEPTH + (z + along) % DEPTH)
        for i in range(sections)
        for z in range(DEPTH)
        if 0 <= i + distance < sections
    ]
    return lax.ppermute(block, ("section", "depth"), route)


def shards(grad_out, gate_probs, routes, saved_preacts, w_gate_up, w_down):
    columns = lax.axis_size("column")
    capacity = saved_preacts.shape[4]
    span = 2 * capacity
    width = grad_out.shape[3]
    tokens = grad_out.shape[2]
    level = lax.axis_index("depth")
    half = level // SHARE
    gate_up = w_gate_up[0, 0]
    down_proj = w_down[0, 0]

    def place(group):
        where = [half] + [(level + DEPTH + offset) % DEPTH for offset in group]
        return jnp.stack(where).astype(jnp.int32)

    picks = jnp.moveaxis(routes[0], 2, 0).reshape(1, 4 * tokens).astype(bf16)
    gates = jnp.moveaxis(gate_probs[0], 2, 0).reshape(1, 4 * tokens)
    line = jnp.concatenate([picks, gates], axis=1)
    own = jnp.concatenate(
        [
            grad_out[0].reshape(2 * tokens, width),
            jnp.pad(line, ((0, META - 1), (0, width - line.shape[1]))),
        ]
    )
    arrivals = {0: own}
    for group in GROUPS[1:]:
        for offset in group:
            toward = 1 if offset < 0 else -1
            arrivals[offset] = hop(arrivals[offset + toward], toward)
    everyone = [arrivals[offset] for group in GROUPS for offset in group]

    preacts = jnp.concatenate([saved_preacts[0, 0, 0], saved_preacts[0, 1, 0]], axis=1)
    preacts = preacts.reshape(columns, DEPTH, span, -1)
    received, sides, hidden, parts = [], [], [], []
    for n, group in enumerate(GROUPS):
        last = group == GROUPS[-1]
        earlier = sides[n - 2 : n - 1] if n >= 2 else [preacts] * n
        sent = pack(
            place(group),
            [arrivals[offset] for offset in group],
            columns,
            capacity,
            everyone if last else (),
            earlier,
        )
        got = exchange(sent)
        received.append(got)
        if not last:
            pieces = prepare(place(group), got, preacts, down_proj)
            sides.append(pieces[0])
            hidden.append(pieces[1])
            parts.append(pieces[2])
    last = received[-1]
    final_hidden, sending = turn(place(GROUPS[-1]), last, preacts, down_proj, gate_up, parts)
    hidden.append(final_hidden)

    first = [sum(len(group) for group in GROUPS[:n]) for n in range(len(GROUPS))]
    part_rows = None
    coming = []
    folded = []
    down_grad = None
    for n in reversed(range(len(GROUPS))):
        group = GROUPS[n]
        returned = exchange(sending)
        if part_rows is None:
            part_rows = returned
        earlier = []
        if n > 0:
            held = list(coming)
            if n == len(GROUPS) - 3:
                down_grad = down_grads(received, hidden, width)
                held.append(down_grad)
            sending = slice_grad(first[n - 1], sides[n - 1], last, gate_up, held)
            earlier = [sending]
        folded = fold(
            place(group),
            first[n],
            part_rows,
            returned,
            [arrivals[offset] for offset in group],
            coming,
            capacity,
            n <= 1,
            earlier,
        )
        along = [-1 if offset < 0 else 1 for offset in group]
        if n > 1:
            coming = [hop(block, way) for block, way in zip(folded, along)]
        elif n == 1:
            coming = [hop(folded[3 * m + 2], way) for m, way in enumerate(along)]
            above = [shifted(folded[3 * m], -1, way) for m, way in enumerate(along)]
            below = [shifted(folded[3 * m + 1], 1, way) for m, way in enumerate(along)]
    above.append(shifted(folded[0], -1))
    below.append(shifted(folded[1], 1))
    from_above = sum(part.astype(f32) for part in above).astype(bf16)
    from_below = sum(part.astype(f32) for part in below).astype(bf16)
    prob_grad = jnp.moveaxis(folded[2][0].astype(f32).reshape(2, 2, tokens), 0, 2)
    return (from_above[None], from_below[None], prob_grad[None], down_grad[None, None])


def solution(mesh):
    sections, slices = mesh.devices.shape
    grid = Mesh(mesh.devices.reshape(sections, slices // DEPTH, DEPTH), ("section", "column", "depth"))
    spread = ("column", "depth")
    in_specs = (
        P("section", None, spread, None),
        P("section", None, spread, None),
        P("section", None, spread, None),
        P("section", None, spread, None, None, None),
        P("section", spread, None, None),
        P("section", spread, None, None),
    )
    out_specs = (
        P("section", spread, None),
        P("section", spread, None),
        P("section", None, spread, None),
        P("section", spread, None, None),
    )
    return jax.shard_map(shards, mesh=grid, in_specs=in_specs, out_specs=out_specs, check_vma=False)
```

```python
import functools

import jax
import jax.numpy as jnp
from jax import lax
from jax.experimental import pallas as pl
from jax.experimental.pallas import tpu as pltpu
from jax.sharding import Mesh, PartitionSpec as P

SHARE = 4
DEPTH = 2 * SHARE
GROUPS = ((0,), (-1, 1), (-2, 2), (-3, 3), (-4,))
EXTRA = 128
HALF = 64
LANES = 128
META = 8
TILE = 512
VMEM_LIMIT = 63 * 1024 * 1024

f32 = jnp.float32
bf16 = jnp.bfloat16
NT = (((1,), (1,)), ((), ()))
TN = (((0,), (0,)), ((), ()))


def tags(rows):
    meta = rows[LANES : LANES + META, : 4 * LANES].astype(f32)
    return [meta[0:1, k * LANES : (k + 1) * LANES] for k in range(4)]


def slot_hits(picks, half, count, capacity):
    ids = (half + 2 * lax.broadcasted_iota(jnp.int32, (count, LANES), 0)).astype(f32)
    named = (picks[0] == ids) | (picks[1] == ids)
    row = lax.broadcasted_iota(jnp.int32, (LANES, LANES), 0)
    col = lax.broadcasted_iota(jnp.int32, (LANES, LANES), 1)
    earlier = (row < col) & (row // HALF == col // HALF)
    before = jnp.dot(
        named.astype(f32).astype(bf16), earlier.astype(f32).astype(bf16), preferred_element_type=f32
    )
    stretch = lax.broadcasted_iota(jnp.int32, (count, LANES), 1) // HALF
    keys = jnp.where(named, before + (stretch * capacity).astype(f32), -1.0)
    slot = lax.broadcasted_iota(jnp.int32, (count, 2 * capacity, LANES), 1).astype(f32)
    return jnp.where(slot == keys[:, None, :], 1.0, 0.0), ids


def flat(hits):
    return hits.reshape(-1, LANES).astype(bf16)


def tiles(width):
    return [slice(low, low + TILE) for low in range(0, width, TILE)]


def read_tile(ref, source, tile):
    share = TILE // ref.shape[4]
    parts = [ref[:, source, tile * share + i] for i in range(share)]
    block = parts[0] if share == 1 else jnp.concatenate(parts, axis=2)
    return block.reshape(block.shape[0] * block.shape[1], TILE)


def write_tile(ref, source, tile, values):
    narrow = ref.shape[4]
    share = TILE // narrow
    block = values.reshape(ref.shape[0], ref.shape[3], TILE)
    for i in range(share):
        ref[:, source, tile * share + i] = block[:, :, i * narrow : (i + 1) * narrow]


def params():
    return pltpu.CompilerParams(vmem_limit_bytes=VMEM_LIMIT)


SMEM = pl.BlockSpec(memory_space=pltpu.SMEM)
VMEM = pl.BlockSpec(memory_space=pltpu.VMEM)
ANY = pl.BlockSpec(memory_space=pl.ANY)


def pack_kernel(capacity, count, tagged, width, place, *refs):
    out = refs[-1]
    columns = out.shape[0]
    for m in range(count):
        rows = refs[m]
        hits, _ = slot_hits(tags(rows), place[0], columns, capacity)
        ones = flat(hits)
        for k, tile in enumerate(tiles(width)):
            packed = jnp.dot(ones, rows[:LANES, tile], preferred_element_type=f32)
            write_tile(out, m, k, packed.astype(bf16))
    if tagged:
        lane = lax.broadcasted_iota(jnp.int32, (columns, 2 * capacity, EXTRA), 2)
        scales = jnp.zeros((columns, 2 * capacity, EXTRA), f32)
        for k, rows in enumerate(refs[count : count + tagged]):
            meta = rows[:, :].astype(f32)
            picks = [meta[0:1, i * LANES : (i + 1) * LANES] for i in range(4)]
            hits, ids = slot_hits(picks, place[0], columns, capacity)
            gates = jnp.where(picks[0] == ids, picks[2], 0.0) + jnp.where(picks[1] == ids, picks[3], 0.0)
            scale = jnp.sum(hits * gates[:, None, :], axis=2, keepdims=True)
            scales = jnp.where(lane == k, scale, scales)
        out[:, 0, out.shape[2] - 1] = scales.astype(bf16)


def pack(place, arrivals, columns, capacity, tagged=(), earlier=()):
    width = arrivals[0].shape[1]
    narrow = EXTRA if tagged else TILE
    pieces = width // narrow + (1 if tagged else 0)
    only_tags = pl.BlockSpec((META, 4 * LANES), lambda i: (LANES // META, 0))
    return pl.pallas_call(
        functools.partial(pack_kernel, capacity, len(arrivals), len(tagged), width),
        out_shape=jax.ShapeDtypeStruct((columns, len(arrivals), pieces, 2 * capacity, narrow), bf16),
        grid=(1,),
        in_specs=[SMEM] + [VMEM] * len(arrivals) + [only_tags] * len(tagged) + [ANY] * len(earlier),
        out_specs=VMEM,
        compiler_params=params(),
        name="pack_rows",
    )(place, *arrivals, *tagged, *earlier)


def expert_parts(received, preacts, down_proj):
    width = down_proj.shape[1]
    half = down_proj.shape[0]
    back = 0.0
    for k, tile in enumerate(tiles(width)):
        back += lax.dot_general(read_tile(received, 0, k), down_proj[:, tile], NT, preferred_element_type=f32)
    gate_pre = preacts[:, :half].astype(f32)
    up_pre = preacts[:, half:].astype(f32)
    sig = 1.0 / (1.0 + jnp.exp(-gate_pre))
    act = gate_pre * sig
    hidden = act * up_pre
    part = jnp.sum(hidden * back, axis=1, keepdims=True)
    gate_side = back * up_pre * sig * (1.0 + gate_pre * (1.0 - sig))
    return gate_side, back * act, hidden, part


def prepare_kernel(place, rows, preacts, down_proj, sides, hidden, parts):
    slots = sides.shape[1]
    half = hidden.shape[2]
    pre = preacts[:, 0].reshape(slots, 2 * half)
    gate_side, up_side, hid, part = expert_parts(rows, pre, down_proj)
    sides[0, :, :half] = gate_side
    sides[0, :, half:] = up_side
    hidden[0] = hid
    parts[0] = jnp.broadcast_to(part, (slots, EXTRA))


def prepare(place, received, preacts, down_proj):
    columns, count, pieces, span, narrow = received.shape
    half, width = down_proj.shape
    slots = columns * span
    block = lambda m, place: (m, 0, 0)
    return pl.pallas_call(
        prepare_kernel,
        out_shape=[
            jax.ShapeDtypeStruct((count, slots, 2 * half), f32),
            jax.ShapeDtypeStruct((count, slots, half), f32),
            jax.ShapeDtypeStruct((count, slots, EXTRA), f32),
        ],
        grid_spec=pltpu.PrefetchScalarGridSpec(
            num_scalar_prefetch=1,
            grid=(count,),
            in_specs=[
                pl.BlockSpec((columns, 1, pieces, span, narrow), lambda m, place: (0, m, 0, 0, 0)),
                pl.BlockSpec((columns, 1, span, 2 * half), lambda m, place: (0, place[1 + m], 0, 0)),
                pl.BlockSpec((half, width), lambda m, place: (0, 0)),
            ],
            out_specs=[
                pl.BlockSpec((1, slots, 2 * half), block),
                pl.BlockSpec((1, slots, half), block),
                pl.BlockSpec((1, slots, EXTRA), block),
            ],
        ),
        compiler_params=params(),
        name="prepare",
    )(place, received, preacts, down_proj)


def turn_kernel(count, place, received, preacts, down_proj, gate_up, *refs):
    others, hidden, out = refs[:-2], refs[-2], refs[-1]
    half, width = down_proj.shape
    columns, _, pieces, span, _ = received.shape
    slots = columns * span
    scales = received[:, 0, pieces - 1].astype(f32).reshape(slots, EXTRA)
    gate_side, up_side, hid, part = expert_parts(received, preacts[:, 0].reshape(slots, 2 * half), down_proj)
    hidden[0] = hid
    scale = scales[:, count - 1 : count]
    both = jnp.concatenate([scale * gate_side, scale * up_side], axis=1).astype(bf16)
    for k, tile in enumerate(tiles(width)):
        grad = lax.dot_general(both, gate_up[tile, :], NT, preferred_element_type=f32)
        write_tile(out, 0, k, grad.astype(bf16))
    lane = lax.broadcasted_iota(jnp.int32, (slots, EXTRA), 1)
    parts = jnp.where(lane == count - 1, part, 0.0)
    k = 0
    for group in others:
        for m in range(group.shape[0]):
            parts = jnp.where(lane == k, group[m], parts)
            k += 1
    out[:, 0, pieces - 1] = parts.astype(bf16).reshape(columns, span, EXTRA)


def turn(place, received, preacts, down_proj, gate_up, parts):
    columns, _, pieces, span, narrow = received.shape
    half, width = down_proj.shape
    slots = columns * span
    count = 1 + sum(p.shape[0] for p in parts)
    return pl.pallas_call(
        functools.partial(turn_kernel, count),
        out_shape=[
            jax.ShapeDtypeStruct((1, slots, half), f32),
            jax.ShapeDtypeStruct((columns, 1, pieces, span, narrow), bf16),
        ],
        grid_spec=pltpu.PrefetchScalarGridSpec(
            num_scalar_prefetch=1,
            grid=(1,),
            in_specs=[
                VMEM,
                pl.BlockSpec((columns, 1, span, 2 * half), lambda m, place: (0, place[1], 0, 0)),
                VMEM,
                VMEM,
            ]
            + [VMEM] * len(parts),
            out_specs=[VMEM, VMEM],
        ),
        compiler_params=params(),
        name="turn",
    )(place, received, preacts, down_proj, gate_up, *parts)


def grad_kernel(first, sides, last, gate_up, *rest):
    out = rest[-1]
    width = gate_up.shape[0]
    columns, _, _, span, _ = out.shape
    slots = columns * span
    scales = last[:, 0, 0].reshape(slots, EXTRA).astype(f32)
    lane = lax.broadcasted_iota(jnp.int32, (slots, EXTRA), 1)
    index = first + pl.program_id(0)
    scale = jnp.sum(jnp.where(lane == index, scales, 0.0), axis=1, keepdims=True)
    both = (scale * sides[0]).astype(bf16)
    for k, tile in enumerate(tiles(width)):
        grad = lax.dot_general(both, gate_up[tile, :], NT, preferred_element_type=f32)
        write_tile(out, 0, k, grad.astype(bf16))


def slice_grad(first, sides, last, gate_up, earlier):
    count, slots, full = sides.shape
    columns, _, _, span, _ = last.shape
    width = gate_up.shape[0]
    pieces = width // TILE
    shape = jax.ShapeDtypeStruct((columns, count, pieces, span, TILE), bf16)
    most = width - TILE
    shared = [
        pl.BlockSpec((1, slots, full), lambda m: (m, 0, 0)),
        pl.BlockSpec((columns, 1, 1, span, EXTRA), lambda m: (0, 0, width // EXTRA, 0, 0)),
    ]
    sending = pl.pallas_call(
        functools.partial(grad_kernel, first),
        out_shape=shape,
        grid=(count,),
        in_specs=shared + [pl.BlockSpec((most, full), lambda m: (0, 0))],
        out_specs=pl.BlockSpec((columns, 1, pieces - 1, span, TILE), lambda m: (0, m, 0, 0, 0)),
        compiler_params=params(),
        name="slice_grad",
    )(sides, last, gate_up)
    return pl.pallas_call(
        functools.partial(grad_kernel, first),
        out_shape=shape,
        grid=(count,),
        in_specs=shared
        + [pl.BlockSpec((TILE, full), lambda m: (most // TILE, 0)), ANY]
        + [ANY] * len(earlier),
        out_specs=pl.BlockSpec((columns, 1, 1, span, TILE), lambda m: (0, m, pieces - 1, 0, 0)),
        input_output_aliases={3: 0},
        compiler_params=params(),
        name="slice_grad_end",
    )(sides, last, gate_up, sending, *earlier)


def down_kernel(groups, last, *refs):
    rows, hidden, out, scaled = refs[:groups], refs[groups : 2 * groups], refs[-2], refs[-1]
    slots = hidden[0].shape[1]

    @pl.when(pl.program_id(0) == 0)
    def _():
        scales = last[:, 0, 0].reshape(slots, EXTRA).astype(f32)
        k = 0
        for group in hidden:
            for m in range(group.shape[0]):
                scaled[k * slots : (k + 1) * slots] = (scales[:, k : k + 1] * group[m]).astype(bf16)
                k += 1

    total = jnp.zeros(out.shape, f32)
    k = 0
    for group in rows:
        for m in range(group.shape[1]):
            table = read_tile(group, m, 0)
            part = scaled[k * slots : (k + 1) * slots]
            total += lax.dot_general(part, table, TN, preferred_element_type=f32)
            k += 1
    out[...] = total.astype(bf16)


def down_grads(received, hidden, width):
    last = received[-1]
    columns, _, _, span, _ = last.shape
    count = sum(h.shape[0] for h in hidden)
    slots, half = hidden[0].shape[1:]
    return pl.pallas_call(
        functools.partial(down_kernel, len(received)),
        out_shape=jax.ShapeDtypeStruct((half, width), bf16),
        grid=(width // TILE,),
        in_specs=[pl.BlockSpec((columns, 1, 1, span, EXTRA), lambda i: (0, 0, width // EXTRA, 0, 0))]
        + [
            pl.BlockSpec((columns, g.shape[1], TILE // g.shape[4], span, g.shape[4]), lambda i: (0, 0, i, 0, 0))
            for g in received
        ]
        + [pl.BlockSpec(h.shape, lambda i: (0, 0, 0)) for h in hidden],
        out_specs=pl.BlockSpec((half, TILE), lambda i: (0, i)),
        scratch_shapes=[pltpu.VMEM((count * slots, half), bf16)],
        compiler_params=params(),
        name="down_grads",
    )(last, *received, *hidden)


def fold_kernel(capacity, first, count, coming, split, place, parts, *refs):
    returned = refs[0]
    metas = refs[1 : 1 + count]
    incoming = refs[1 + count : 1 + count + coming]
    outs = refs[-3 * count :] if split else refs[-count:]
    columns, _, pieces, span, narrow = returned.shape
    table = parts[:, 0, 0].astype(f32)
    for m in range(count):
        meta = metas[m][:, :].astype(f32)
        picks = [meta[0:1, i * LANES : (i + 1) * LANES] for i in range(4)]
        hits, ids = slot_hits(picks, place[0], columns, capacity)
        ones = flat(hits)
        added = incoming[m::count] if coming >= count else incoming[m : m + 1]
        sums = [other for other in added if other.shape[0] > META]
        for n, tile in enumerate(tiles(pieces * narrow // TILE * TILE)):
            total = lax.dot_general(ones, read_tile(returned, m, n), TN, preferred_element_type=f32)
            for other in sums:
                total = total + other[:LANES, tile].astype(f32)
            total = total.astype(bf16)
            if split:
                outs[3 * m][:, tile] = total[:HALF]
                outs[3 * m + 1][:, tile] = total[HALF:]
            else:
                outs[m][:LANES, tile] = total
        values = hits * table[:, :, first + m : first + m + 1]
        for k in range(2):
            named = jnp.where(picks[k] == ids, 1.0, 0.0)[:, None, :]
            line = jnp.sum(jnp.sum(values * named, axis=1), axis=0, keepdims=True)
            lanes = slice(k * LANES, (k + 1) * LANES)
            for other in added:
                low = LANES if other.shape[0] > META else 0
                line = line + other[low : low + META, lanes].astype(f32)[0:1]
            line = jnp.broadcast_to(line, (META, LANES)).astype(bf16)
            if split:
                outs[3 * m + 2][:, lanes] = line
            else:
                outs[m][LANES : LANES + META, lanes] = line


def fold(place, first, parts, returned, arrivals, incoming, capacity, split, earlier=()):
    columns, count, _, span, _ = returned.shape
    width = arrivals[0].shape[1]
    only_tags = pl.BlockSpec((META, 4 * LANES), lambda i: (LANES // META, 0))
    if split:
        halves = [jax.ShapeDtypeStruct((HALF, width), bf16)] * 2
        shapes = (halves + [jax.ShapeDtypeStruct((META, 2 * LANES), bf16)]) * count
    else:
        shapes = [jax.ShapeDtypeStruct((LANES + META, width), bf16)] * count
    return pl.pallas_call(
        functools.partial(fold_kernel, capacity, first, count, len(incoming), split),
        out_shape=shapes,
        grid=(1,),
        in_specs=[SMEM, pl.BlockSpec((columns, 1, 1, span, EXTRA), lambda i: (0, 0, width // EXTRA, 0, 0)), VMEM]
        + [only_tags] * count
        + [VMEM] * len(incoming)
        + [ANY] * len(earlier),
        out_specs=[VMEM] * len(shapes),
        compiler_params=params(),
        name="fold_rows",
    )(place, parts, returned, *arrivals, *incoming, *earlier)


def exchange(block):
    columns, count, pieces, span, narrow = block.shape
    merged = block.reshape(columns, count * pieces, span, narrow)
    moved = lax.all_to_all(merged, "column", split_axis=0, concat_axis=0, tiled=True)
    return moved.reshape(block.shape)


def hop(block, distance):
    return lax.ppermute(block, "depth", [(i, (i + distance) % DEPTH) for i in range(DEPTH)])


def shifted(block, distance, along=0):
    sections = lax.axis_size("section")
    route = [
        (i * DEPTH + z, (i + distance) * DEPTH + (z + along) % DEPTH)
        for i in range(sections)
        for z in range(DEPTH)
        if 0 <= i + distance < sections
    ]
    return lax.ppermute(block, ("section", "depth"), route)


def shards(grad_out, gate_probs, routes, saved_preacts, w_gate_up, w_down):
    columns = lax.axis_size("column")
    capacity = saved_preacts.shape[4]
    span = 2 * capacity
    width = grad_out.shape[3]
    tokens = grad_out.shape[2]
    level = lax.axis_index("depth")
    half = level // SHARE
    gate_up = w_gate_up[0, 0]
    down_proj = w_down[0, 0]

    def place(group):
        where = [half] + [(level + DEPTH + offset) % DEPTH for offset in group]
        return jnp.stack(where).astype(jnp.int32)

    picks = jnp.moveaxis(routes[0], 2, 0).reshape(1, 4 * tokens).astype(bf16)
    gates = jnp.moveaxis(gate_probs[0], 2, 0).reshape(1, 4 * tokens)
    line = jnp.concatenate([picks, gates], axis=1)
    own = jnp.concatenate(
        [
            grad_out[0].reshape(2 * tokens, width),
            jnp.pad(line, ((0, META - 1), (0, width - line.shape[1]))),
        ]
    )
    arrivals = {0: own}
    for group in GROUPS[1:]:
        for offset in group:
            toward = 1 if offset < 0 else -1
            arrivals[offset] = hop(arrivals[offset + toward], toward)
    everyone = [arrivals[offset] for group in GROUPS for offset in group]

    preacts = jnp.concatenate([saved_preacts[0, 0, 0], saved_preacts[0, 1, 0]], axis=1)
    preacts = preacts.reshape(columns, DEPTH, span, -1)
    received, sides, hidden, parts = [], [], [], []
    for n, group in enumerate(GROUPS):
        last = group == GROUPS[-1]
        earlier = sides[n - 2 : n - 1] if n >= 2 else [preacts] * n
        sent = pack(
            place(group),
            [arrivals[offset] for offset in group],
            columns,
            capacity,
            everyone if last else (),
            earlier,
        )
        got = exchange(sent)
        received.append(got)
        if not last:
            pieces = prepare(place(group), got, preacts, down_proj)
            sides.append(pieces[0])
            hidden.append(pieces[1])
            parts.append(pieces[2])
    last = received[-1]
    final_hidden, sending = turn(place(GROUPS[-1]), last, preacts, down_proj, gate_up, parts)
    hidden.append(final_hidden)

    first = [sum(len(group) for group in GROUPS[:n]) for n in range(len(GROUPS))]
    part_rows = None
    coming = []
    folded = []
    down_grad = None
    for n in reversed(range(len(GROUPS))):
        group = GROUPS[n]
        returned = exchange(sending)
        if part_rows is None:
            part_rows = returned
        earlier = []
        if n > 0:
            held = list(coming)
            if n == len(GROUPS) - 3:
                down_grad = down_grads(received, hidden, width)
                held.append(down_grad)
            sending = slice_grad(first[n - 1], sides[n - 1], last, gate_up, held)
            earlier = [sending]
        folded = fold(
            place(group),
            first[n],
            part_rows,
            returned,
            [arrivals[offset] for offset in group],
            coming,
            capacity,
            n <= 1,
            earlier,
        )
        along = [-1 if offset < 0 else 1 for offset in group]
        if n > 1:
            coming = [hop(block, way) for block, way in zip(folded, along)]
        elif n == 1:
            coming = [hop(folded[3 * m + 2], way) for m, way in enumerate(along)]
            above = [shifted(folded[3 * m], -1, way) for m, way in enumerate(along)]
            below = [shifted(folded[3 * m + 1], 1, way) for m, way in enumerate(along)]
    above.append(shifted(folded[0], -1))
    below.append(shifted(folded[1], 1))
    from_above = sum(part.astype(f32) for part in above).astype(bf16)
    from_below = sum(part.astype(f32) for part in below).astype(bf16)
    prob_grad = jnp.moveaxis(folded[2][0].astype(f32).reshape(2, 2, tokens), 0, 2)
    return (from_above[None], from_below[None], prob_grad[None], down_grad[None, None])


def solution(mesh):
    sections, slices = mesh.devices.shape
    grid = Mesh(mesh.devices.reshape(sections, slices // DEPTH, DEPTH), ("section", "column", "depth"))
    spread = ("column", "depth")
    in_specs = (
        P("section", None, spread, None),
        P("section", None, spread, None),
        P("section", None, spread, None),
        P("section", None, spread, None, None, None),
        P("section", spread, None, None),
        P("section", spread, None, None),
    )
    out_specs = (
        P("section", spread, None),
        P("section", spread, None),
        P("section", None, spread, None),
        P("section", spread, None, None),
    )
    return jax.shard_map(shards, mesh=grid, in_specs=in_specs, out_specs=out_specs, check_vma=False)
```

```python
import functools

import jax
import jax.numpy as jnp
from jax import lax
from jax.experimental import pallas as pl
from jax.experimental.pallas import tpu as pltpu
from jax.sharding import Mesh, PartitionSpec as P

SHARE = 4
DEPTH = 2 * SHARE
GROUPS = ((0, -1, 1), (-2, 2), (-3, 3), (-4,))
BACK = ((-4,), (-3, 3), (-2, 2), (-1, 1), (0,))
EXTRA = 128
HALF = 64
LANES = 128
META = 8
TILE = 512
VMEM_LIMIT = 63 * 1024 * 1024

f32 = jnp.float32
bf16 = jnp.bfloat16
NT = (((1,), (1,)), ((), ()))
TN = (((0,), (0,)), ((), ()))


def tags(rows):
    meta = rows[LANES : LANES + META, : 4 * LANES].astype(f32)
    return [meta[0:1, k * LANES : (k + 1) * LANES] for k in range(4)]


def slot_hits(picks, half, count, capacity):
    ids = (half + 2 * lax.broadcasted_iota(jnp.int32, (count, LANES), 0)).astype(f32)
    named = (picks[0] == ids) | (picks[1] == ids)
    row = lax.broadcasted_iota(jnp.int32, (LANES, LANES), 0)
    col = lax.broadcasted_iota(jnp.int32, (LANES, LANES), 1)
    earlier = (row < col) & (row // HALF == col // HALF)
    before = jnp.dot(
        named.astype(f32).astype(bf16), earlier.astype(f32).astype(bf16), preferred_element_type=f32
    )
    stretch = lax.broadcasted_iota(jnp.int32, (count, LANES), 1) // HALF
    keys = jnp.where(named, before + (stretch * capacity).astype(f32), -1.0)
    slot = lax.broadcasted_iota(jnp.int32, (count, 2 * capacity, LANES), 1).astype(f32)
    return jnp.where(slot == keys[:, None, :], 1.0, 0.0), ids


def flat(hits):
    return hits.reshape(-1, LANES).astype(bf16)


def tiles(width):
    return [slice(low, low + TILE) for low in range(0, width, TILE)]


def read_tile(ref, source, tile):
    share = TILE // ref.shape[4]
    parts = [ref[:, source, tile * share + i] for i in range(share)]
    block = parts[0] if share == 1 else jnp.concatenate(parts, axis=2)
    return block.reshape(block.shape[0] * block.shape[1], TILE)


def write_tile(ref, source, tile, values):
    narrow = ref.shape[4]
    share = TILE // narrow
    block = values.reshape(ref.shape[0], ref.shape[3], TILE)
    for i in range(share):
        ref[:, source, tile * share + i] = block[:, :, i * narrow : (i + 1) * narrow]


def params():
    return pltpu.CompilerParams(vmem_limit_bytes=VMEM_LIMIT)


SMEM = pl.BlockSpec(memory_space=pltpu.SMEM)
VMEM = pl.BlockSpec(memory_space=pltpu.VMEM)
ANY = pl.BlockSpec(memory_space=pl.ANY)


def ordered(block, *others):
    return pl.pallas_call(
        lambda *refs: None,
        out_shape=jax.ShapeDtypeStruct(block.shape, block.dtype),
        in_specs=[ANY] * (1 + len(others)),
        out_specs=ANY,
        input_output_aliases={0: 0},
        name="ordered",
    )(block, *others)


def pack_kernel(capacity, count, tagged, width, place, *refs):
    out = refs[-1]
    columns = out.shape[0]
    for m in range(count):
        rows = refs[m]
        hits, _ = slot_hits(tags(rows), place[0], columns, capacity)
        ones = flat(hits)
        for k, tile in enumerate(tiles(width)):
            packed = jnp.dot(ones, rows[:LANES, tile], preferred_element_type=f32)
            write_tile(out, m, k, packed.astype(bf16))
    if tagged:
        lane = lax.broadcasted_iota(jnp.int32, (columns, 2 * capacity, EXTRA), 2)
        scales = jnp.zeros((columns, 2 * capacity, EXTRA), f32)
        for k, rows in enumerate(refs[count : count + tagged]):
            meta = rows[:, :].astype(f32)
            picks = [meta[0:1, i * LANES : (i + 1) * LANES] for i in range(4)]
            hits, ids = slot_hits(picks, place[0], columns, capacity)
            gates = jnp.where(picks[0] == ids, picks[2], 0.0) + jnp.where(picks[1] == ids, picks[3], 0.0)
            scale = jnp.sum(hits * gates[:, None, :], axis=2, keepdims=True)
            scales = jnp.where(lane == k, scale, scales)
        out[:, 0, out.shape[2] - 1] = scales.astype(bf16)


def pack(place, arrivals, columns, capacity, tagged=(), earlier=()):
    width = arrivals[0].shape[1]
    narrow = EXTRA if tagged else TILE
    pieces = width // narrow + (1 if tagged else 0)
    only_tags = pl.BlockSpec((META, 4 * LANES), lambda i: (LANES // META, 0))
    return pl.pallas_call(
        functools.partial(pack_kernel, capacity, len(arrivals), len(tagged), width),
        out_shape=jax.ShapeDtypeStruct((columns, len(arrivals), pieces, 2 * capacity, narrow), bf16),
        grid=(1,),
        in_specs=[SMEM] + [VMEM] * len(arrivals) + [only_tags] * len(tagged) + [ANY] * len(earlier),
        out_specs=VMEM,
        compiler_params=params(),
        name="pack_rows",
    )(place, *arrivals, *tagged, *earlier)


def expert_parts(received, preacts, down_proj):
    width = down_proj.shape[1]
    half = down_proj.shape[0]
    back = 0.0
    for k, tile in enumerate(tiles(width)):
        back += lax.dot_general(read_tile(received, 0, k), down_proj[:, tile], NT, preferred_element_type=f32)
    gate_pre = preacts[:, :half].astype(f32)
    up_pre = preacts[:, half:].astype(f32)
    sig = 1.0 / (1.0 + jnp.exp(-gate_pre))
    act = gate_pre * sig
    hidden = act * up_pre
    part = jnp.sum(hidden * back, axis=1, keepdims=True)
    gate_side = back * up_pre * sig * (1.0 + gate_pre * (1.0 - sig))
    return gate_side, back * act, hidden, part


def prepare_kernel(place, rows, preacts, down_proj, sides, hidden, parts):
    slots = sides.shape[1]
    half = hidden.shape[2]
    pre = preacts[:, 0].reshape(slots, 2 * half)
    gate_side, up_side, hid, part = expert_parts(rows, pre, down_proj)
    sides[0, :, :half] = gate_side
    sides[0, :, half:] = up_side
    hidden[0] = hid
    parts[0] = jnp.broadcast_to(part, (slots, EXTRA))


def prepare(place, received, preacts, down_proj):
    columns, count, pieces, span, narrow = received.shape
    half, width = down_proj.shape
    slots = columns * span
    block = lambda m, place: (m, 0, 0)
    return pl.pallas_call(
        prepare_kernel,
        out_shape=[
            jax.ShapeDtypeStruct((count, slots, 2 * half), f32),
            jax.ShapeDtypeStruct((count, slots, half), f32),
            jax.ShapeDtypeStruct((count, slots, EXTRA), f32),
        ],
        grid_spec=pltpu.PrefetchScalarGridSpec(
            num_scalar_prefetch=1,
            grid=(count,),
            in_specs=[
                pl.BlockSpec((columns, 1, pieces, span, narrow), lambda m, place: (0, m, 0, 0, 0)),
                pl.BlockSpec((columns, 1, span, 2 * half), lambda m, place: (0, place[1 + m], 0, 0)),
                pl.BlockSpec((half, width), lambda m, place: (0, 0)),
            ],
            out_specs=[
                pl.BlockSpec((1, slots, 2 * half), block),
                pl.BlockSpec((1, slots, half), block),
                pl.BlockSpec((1, slots, EXTRA), block),
            ],
        ),
        compiler_params=params(),
        name="prepare",
    )(place, received, preacts, down_proj)


def turn_kernel(count, place, received, preacts, down_proj, gate_up, *refs):
    others, hidden, out = refs[:-2], refs[-2], refs[-1]
    half, width = down_proj.shape
    columns, _, pieces, span, _ = received.shape
    slots = columns * span
    scales = received[:, 0, pieces - 1].astype(f32).reshape(slots, EXTRA)
    gate_side, up_side, hid, part = expert_parts(received, preacts[:, 0].reshape(slots, 2 * half), down_proj)
    hidden[0] = hid
    scale = scales[:, count - 1 : count]
    both = jnp.concatenate([scale * gate_side, scale * up_side], axis=1).astype(bf16)
    for k, tile in enumerate(tiles(width)):
        grad = lax.dot_general(both, gate_up[tile, :], NT, preferred_element_type=f32)
        write_tile(out, 0, k, grad.astype(bf16))
    lane = lax.broadcasted_iota(jnp.int32, (slots, EXTRA), 1)
    parts = jnp.where(lane == count - 1, part, 0.0)
    k = 0
    for group in others:
        for m in range(group.shape[0]):
            parts = jnp.where(lane == k, group[m], parts)
            k += 1
    out[:, 0, pieces - 1] = parts.astype(bf16).reshape(columns, span, EXTRA)


def turn(place, received, preacts, down_proj, gate_up, parts):
    columns, _, pieces, span, narrow = received.shape
    half, width = down_proj.shape
    slots = columns * span
    count = 1 + sum(p.shape[0] for p in parts)
    return pl.pallas_call(
        functools.partial(turn_kernel, count),
        out_shape=[
            jax.ShapeDtypeStruct((1, slots, half), f32),
            jax.ShapeDtypeStruct((columns, 1, pieces, span, narrow), bf16),
        ],
        grid_spec=pltpu.PrefetchScalarGridSpec(
            num_scalar_prefetch=1,
            grid=(1,),
            in_specs=[
                VMEM,
                pl.BlockSpec((columns, 1, span, 2 * half), lambda m, place: (0, place[1], 0, 0)),
                VMEM,
                VMEM,
            ]
            + [VMEM] * len(parts),
            out_specs=[VMEM, VMEM],
        ),
        compiler_params=params(),
        name="turn",
    )(place, received, preacts, down_proj, gate_up, *parts)


def grad_kernel(first, sides, last, gate_up, *rest):
    out = rest[-1]
    width = gate_up.shape[0]
    columns, _, _, span, _ = out.shape
    slots = columns * span
    scales = last[:, 0, 0].reshape(slots, EXTRA).astype(f32)
    lane = lax.broadcasted_iota(jnp.int32, (slots, EXTRA), 1)
    index = first + pl.program_id(0)
    scale = jnp.sum(jnp.where(lane == index, scales, 0.0), axis=1, keepdims=True)
    both = (scale * sides[0]).astype(bf16)
    for k, tile in enumerate(tiles(width)):
        grad = lax.dot_general(both, gate_up[tile, :], NT, preferred_element_type=f32)
        write_tile(out, 0, k, grad.astype(bf16))


def slice_grad(first, offset, count, sides, last, gate_up):
    _, slots, full = sides.shape
    columns, _, _, span, _ = last.shape
    width = gate_up.shape[0]
    pieces = width // TILE
    return pl.pallas_call(
        functools.partial(grad_kernel, first),
        out_shape=jax.ShapeDtypeStruct((columns, count, pieces, span, TILE), bf16),
        grid=(count,),
        in_specs=[
            pl.BlockSpec((1, slots, full), lambda m: (offset + m, 0, 0)),
            pl.BlockSpec((columns, 1, 1, span, EXTRA), lambda m: (0, 0, width // EXTRA, 0, 0)),
            pl.BlockSpec((width, full), lambda m: (0, 0)),
        ],
        out_specs=pl.BlockSpec((columns, 1, pieces, span, TILE), lambda m: (0, m, 0, 0, 0)),
        compiler_params=params(),
        name="slice_grad",
    )(sides, last, gate_up)


def down_kernel(groups, last, *refs):
    rows, hidden, out, scaled = refs[:groups], refs[groups : 2 * groups], refs[-2], refs[-1]
    slots = hidden[0].shape[1]

    @pl.when(pl.program_id(0) == 0)
    def _():
        scales = last[:, 0, 0].reshape(slots, EXTRA).astype(f32)
        k = 0
        for group in hidden:
            for m in range(group.shape[0]):
                scaled[k * slots : (k + 1) * slots] = (scales[:, k : k + 1] * group[m]).astype(bf16)
                k += 1

    total = jnp.zeros(out.shape, f32)
    k = 0
    for group in rows:
        for m in range(group.shape[1]):
            table = read_tile(group, m, 0)
            part = scaled[k * slots : (k + 1) * slots]
            total += lax.dot_general(part, table, TN, preferred_element_type=f32)
            k += 1
    out[...] = total.astype(bf16)


def down_grads(received, hidden, width):
    last = received[-1]
    columns, _, _, span, _ = last.shape
    count = sum(h.shape[0] for h in hidden)
    slots, half = hidden[0].shape[1:]
    return pl.pallas_call(
        functools.partial(down_kernel, len(received)),
        out_shape=jax.ShapeDtypeStruct((half, width), bf16),
        grid=(width // TILE,),
        in_specs=[pl.BlockSpec((columns, 1, 1, span, EXTRA), lambda i: (0, 0, width // EXTRA, 0, 0))]
        + [
            pl.BlockSpec((columns, g.shape[1], TILE // g.shape[4], span, g.shape[4]), lambda i: (0, 0, i, 0, 0))
            for g in received
        ]
        + [pl.BlockSpec(h.shape, lambda i: (0, 0, 0)) for h in hidden],
        out_specs=pl.BlockSpec((half, TILE), lambda i: (0, i)),
        scratch_shapes=[pltpu.VMEM((count * slots, half), bf16)],
        compiler_params=params(),
        name="down_grads",
    )(last, *received, *hidden)


def fold_kernel(capacity, first, count, coming, split, place, parts, *refs):
    returned = refs[0]
    metas = refs[1 : 1 + count]
    incoming = refs[1 + count : 1 + count + coming]
    outs = refs[-3 * count :] if split else refs[-count:]
    columns, _, pieces, span, narrow = returned.shape
    table = parts[:, 0, 0].astype(f32)
    for m in range(count):
        meta = metas[m][:, :].astype(f32)
        picks = [meta[0:1, i * LANES : (i + 1) * LANES] for i in range(4)]
        hits, ids = slot_hits(picks, place[0], columns, capacity)
        ones = flat(hits)
        added = incoming[m::count] if coming >= count else incoming[m : m + 1]
        sums = [other for other in added if other.shape[0] > META]
        for n, tile in enumerate(tiles(pieces * narrow // TILE * TILE)):
            total = lax.dot_general(ones, read_tile(returned, m, n), TN, preferred_element_type=f32)
            for other in sums:
                total = total + other[:LANES, tile].astype(f32)
            total = total.astype(bf16)
            if split:
                outs[3 * m][:, tile] = total[:HALF]
                outs[3 * m + 1][:, tile] = total[HALF:]
            else:
                outs[m][:LANES, tile] = total
        values = hits * table[:, :, first + m : first + m + 1]
        for k in range(2):
            named = jnp.where(picks[k] == ids, 1.0, 0.0)[:, None, :]
            line = jnp.sum(jnp.sum(values * named, axis=1), axis=0, keepdims=True)
            lanes = slice(k * LANES, (k + 1) * LANES)
            for other in added:
                low = LANES if other.shape[0] > META else 0
                line = line + other[low : low + META, lanes].astype(f32)[0:1]
            line = jnp.broadcast_to(line, (META, LANES)).astype(bf16)
            if split:
                outs[3 * m + 2][:, lanes] = line
            else:
                outs[m][LANES : LANES + META, lanes] = line


def fold(place, first, parts, returned, arrivals, incoming, capacity, split, earlier=()):
    columns, count, _, span, _ = returned.shape
    width = arrivals[0].shape[1]
    only_tags = pl.BlockSpec((META, 4 * LANES), lambda i: (LANES // META, 0))
    if split:
        halves = [jax.ShapeDtypeStruct((HALF, width), bf16)] * 2
        shapes = (halves + [jax.ShapeDtypeStruct((META, 2 * LANES), bf16)]) * count
    else:
        shapes = [jax.ShapeDtypeStruct((LANES + META, width), bf16)] * count
    return pl.pallas_call(
        functools.partial(fold_kernel, capacity, first, count, len(incoming), split),
        out_shape=shapes,
        grid=(1,),
        in_specs=[SMEM, pl.BlockSpec((columns, 1, 1, span, EXTRA), lambda i: (0, 0, width // EXTRA, 0, 0)), VMEM]
        + [only_tags] * count
        + [VMEM] * len(incoming)
        + [ANY] * len(earlier),
        out_specs=[VMEM] * len(shapes),
        compiler_params=params(),
        name="fold_rows",
    )(place, parts, returned, *arrivals, *incoming, *earlier)


def exchange(block):
    columns, count, pieces, span, narrow = block.shape
    merged = block.reshape(columns, count * pieces, span, narrow)
    moved = lax.all_to_all(merged, "column", split_axis=0, concat_axis=0, tiled=True)
    return moved.reshape(block.shape)


def hop(block, distance):
    return lax.ppermute(block, "depth", [(i, (i + distance) % DEPTH) for i in range(DEPTH)])


def shifted(block, distance, along=0):
    sections = lax.axis_size("section")
    route = [
        (i * DEPTH + z, (i + distance) * DEPTH + (z + along) % DEPTH)
        for i in range(sections)
        for z in range(DEPTH)
        if 0 <= i + distance < sections
    ]
    return lax.ppermute(block, ("section", "depth"), route)


def shards(grad_out, gate_probs, routes, saved_preacts, w_gate_up, w_down):
    columns = lax.axis_size("column")
    capacity = saved_preacts.shape[4]
    span = 2 * capacity
    width = grad_out.shape[3]
    tokens = grad_out.shape[2]
    level = lax.axis_index("depth")
    half = level // SHARE
    gate_up = w_gate_up[0, 0]
    down_proj = w_down[0, 0]

    def place(group):
        where = [half] + [(level + DEPTH + offset) % DEPTH for offset in group]
        return jnp.stack(where).astype(jnp.int32)

    picks = jnp.moveaxis(routes[0], 2, 0).reshape(1, 4 * tokens).astype(bf16)
    gates = jnp.moveaxis(gate_probs[0], 2, 0).reshape(1, 4 * tokens)
    line = jnp.concatenate([picks, gates], axis=1)
    own = jnp.concatenate(
        [
            grad_out[0].reshape(2 * tokens, width),
            jnp.pad(line, ((0, META - 1), (0, width - line.shape[1]))),
        ]
    )
    arrivals = {0: own}
    for group in reversed(BACK[:-1]):
        for offset in group:
            toward = 1 if offset < 0 else -1
            arrivals[offset] = hop(arrivals[offset + toward], toward)
    everyone = [arrivals[offset] for group in GROUPS for offset in group]

    preacts = jnp.concatenate([saved_preacts[0, 0, 0], saved_preacts[0, 1, 0]], axis=1)
    preacts = preacts.reshape(columns, DEPTH, span, -1)
    received, sides, hidden, parts = [], [], [], []
    for n, group in enumerate(GROUPS):
        last = group == GROUPS[-1]
        earlier = sides[n - 2 : n - 1] if n >= 2 else [preacts] * n
        sent = pack(
            place(group),
            [arrivals[offset] for offset in group],
            columns,
            capacity,
            everyone if last else (),
            earlier,
        )
        if 1 <= n < len(GROUPS) - 1:
            sent = ordered(sent, *[arrivals[offset] for offset in GROUPS[n + 1]])
        got = exchange(sent)
        received.append(got)
        if not last:
            pieces = prepare(place(group), got, preacts, down_proj)
            sides.append(pieces[0])
            hidden.append(pieces[1])
            parts.append(pieces[2])
    last = received[-1]
    final_hidden, sending = turn(place(GROUPS[-1]), last, preacts, down_proj, gate_up, parts)
    hidden.append(final_hidden)

    listed = [offset for group in GROUPS for offset in group]
    part_rows = None
    coming = []
    for n, group in enumerate(BACK):
        returned = exchange(sending)
        if part_rows is None:
            part_rows = returned
        earlier = []
        if n + 1 < len(BACK):
            following = BACK[n + 1]
            start = listed.index(following[0])
            source = [following[0] in g for g in GROUPS].index(True)
            held = list(coming)
            if n == 2:
                down_grad = down_grads(received, hidden, width)
                held.append(down_grad)
            sending = slice_grad(
                start,
                GROUPS[source].index(following[0]),
                len(following),
                sides[source],
                last,
                gate_up,
            )
            sending = ordered(sending, *held) if held else sending
            earlier = [sending]
        folded = fold(
            place(group),
            listed.index(group[0]),
            part_rows,
            returned,
            [arrivals[offset] for offset in group],
            coming,
            capacity,
            n >= len(BACK) - 2,
            earlier,
        )
        along = [-1 if offset < 0 else 1 for offset in group]
        if n < len(BACK) - 2:
            coming = [hop(block, way) for block, way in zip(folded, along)]
        elif n == len(BACK) - 2:
            coming = [hop(folded[3 * m + 2], way) for m, way in enumerate(along)]
            above = [shifted(folded[3 * m], -1, way) for m, way in enumerate(along)]
            below = [shifted(folded[3 * m + 1], 1, way) for m, way in enumerate(along)]
    above.append(shifted(folded[0], -1))
    below.append(shifted(folded[1], 1))
    from_above = sum(part.astype(f32) for part in above).astype(bf16)
    from_below = sum(part.astype(f32) for part in below).astype(bf16)
    prob_grad = jnp.moveaxis(folded[2][0].astype(f32).reshape(2, 2, tokens), 0, 2)
    return (from_above[None], from_below[None], prob_grad[None], down_grad[None, None])


def solution(mesh):
    sections, slices = mesh.devices.shape
    grid = Mesh(mesh.devices.reshape(sections, slices // DEPTH, DEPTH), ("section", "column", "depth"))
    spread = ("column", "depth")
    in_specs = (
        P("section", None, spread, None),
        P("section", None, spread, None),
        P("section", None, spread, None),
        P("section", None, spread, None, None, None),
        P("section", spread, None, None),
        P("section", spread, None, None),
    )
    out_specs = (
        P("section", spread, None),
        P("section", spread, None),
        P("section", None, spread, None),
        P("section", spread, None, None),
    )
    return jax.shard_map(shards, mesh=grid, in_specs=in_specs, out_specs=out_specs, check_vma=False)
```

```python
import functools

import jax
import jax.numpy as jnp
from jax import lax
from jax.experimental import pallas as pl
from jax.experimental.pallas import tpu as pltpu
from jax.sharding import Mesh, PartitionSpec as P

SHARE = 4
DEPTH = 2 * SHARE
GROUPS = ((0,), (-1, 1), (-2, 2), (-3, 3), (-4,))
BACK = ((-4,), (-3, 3), (-2, 2), (-1, 1), (0,))
EXTRA = 128
HALF = 64
LANES = 128
META = 8
TILE = 512
VMEM_LIMIT = 63 * 1024 * 1024

f32 = jnp.float32
bf16 = jnp.bfloat16
NT = (((1,), (1,)), ((), ()))
TN = (((0,), (0,)), ((), ()))


def tags(rows):
    meta = rows[LANES : LANES + META, : 4 * LANES].astype(f32)
    return [meta[0:1, k * LANES : (k + 1) * LANES] for k in range(4)]


def slot_hits(picks, half, count, capacity):
    ids = (half + 2 * lax.broadcasted_iota(jnp.int32, (count, LANES), 0)).astype(f32)
    named = (picks[0] == ids) | (picks[1] == ids)
    row = lax.broadcasted_iota(jnp.int32, (LANES, LANES), 0)
    col = lax.broadcasted_iota(jnp.int32, (LANES, LANES), 1)
    earlier = (row < col) & (row // HALF == col // HALF)
    before = jnp.dot(
        named.astype(f32).astype(bf16), earlier.astype(f32).astype(bf16), preferred_element_type=f32
    )
    stretch = lax.broadcasted_iota(jnp.int32, (count, LANES), 1) // HALF
    keys = jnp.where(named, before + (stretch * capacity).astype(f32), -1.0)
    slot = lax.broadcasted_iota(jnp.int32, (count, 2 * capacity, LANES), 1).astype(f32)
    return jnp.where(slot == keys[:, None, :], 1.0, 0.0), ids


def flat(hits):
    return hits.reshape(-1, LANES).astype(bf16)


def tiles(width):
    return [slice(low, low + TILE) for low in range(0, width, TILE)]


def read_tile(ref, source, tile):
    share = TILE // ref.shape[4]
    parts = [ref[:, source, tile * share + i] for i in range(share)]
    block = parts[0] if share == 1 else jnp.concatenate(parts, axis=2)
    return block.reshape(block.shape[0] * block.shape[1], TILE)


def write_tile(ref, source, tile, values):
    narrow = ref.shape[4]
    share = TILE // narrow
    block = values.reshape(ref.shape[0], ref.shape[3], TILE)
    for i in range(share):
        ref[:, source, tile * share + i] = block[:, :, i * narrow : (i + 1) * narrow]


def params():
    return pltpu.CompilerParams(vmem_limit_bytes=VMEM_LIMIT)


SMEM = pl.BlockSpec(memory_space=pltpu.SMEM)
VMEM = pl.BlockSpec(memory_space=pltpu.VMEM)
ANY = pl.BlockSpec(memory_space=pl.ANY)


def ordered(block, *others):
    return pl.pallas_call(
        lambda *refs: None,
        out_shape=jax.ShapeDtypeStruct(block.shape, block.dtype),
        in_specs=[ANY] * (1 + len(others)),
        out_specs=ANY,
        input_output_aliases={0: 0},
        name="ordered",
    )(block, *others)


def pack_kernel(capacity, count, tagged, width, place, *refs):
    out = refs[-1]
    columns = out.shape[0]
    for m in range(count):
        rows = refs[m]
        hits, _ = slot_hits(tags(rows), place[0], columns, capacity)
        ones = flat(hits)
        for k, tile in enumerate(tiles(width)):
            packed = jnp.dot(ones, rows[:LANES, tile], preferred_element_type=f32)
            write_tile(out, m, k, packed.astype(bf16))
    if tagged:
        lane = lax.broadcasted_iota(jnp.int32, (columns, 2 * capacity, EXTRA), 2)
        scales = jnp.zeros((columns, 2 * capacity, EXTRA), f32)
        for k, rows in enumerate(refs[count : count + tagged]):
            meta = rows[:, :].astype(f32)
            picks = [meta[0:1, i * LANES : (i + 1) * LANES] for i in range(4)]
            hits, ids = slot_hits(picks, place[0], columns, capacity)
            gates = jnp.where(picks[0] == ids, picks[2], 0.0) + jnp.where(picks[1] == ids, picks[3], 0.0)
            scale = jnp.sum(hits * gates[:, None, :], axis=2, keepdims=True)
            scales = jnp.where(lane == k, scale, scales)
        out[:, 0, out.shape[2] - 1] = scales.astype(bf16)


def pack(place, arrivals, columns, capacity, tagged=(), earlier=()):
    width = arrivals[0].shape[1]
    narrow = EXTRA if tagged else TILE
    pieces = width // narrow + (1 if tagged else 0)
    only_tags = pl.BlockSpec((META, 4 * LANES), lambda i: (LANES // META, 0))
    return pl.pallas_call(
        functools.partial(pack_kernel, capacity, len(arrivals), len(tagged), width),
        out_shape=jax.ShapeDtypeStruct((columns, len(arrivals), pieces, 2 * capacity, narrow), bf16),
        grid=(1,),
        in_specs=[SMEM] + [VMEM] * len(arrivals) + [only_tags] * len(tagged) + [ANY] * len(earlier),
        out_specs=VMEM,
        compiler_params=params(),
        name="pack_rows",
    )(place, *arrivals, *tagged, *earlier)


def expert_parts(received, preacts, down_proj):
    width = down_proj.shape[1]
    half = down_proj.shape[0]
    back = 0.0
    for k, tile in enumerate(tiles(width)):
        back += lax.dot_general(read_tile(received, 0, k), down_proj[:, tile], NT, preferred_element_type=f32)
    gate_pre = preacts[:, :half].astype(f32)
    up_pre = preacts[:, half:].astype(f32)
    sig = 1.0 / (1.0 + jnp.exp(-gate_pre))
    act = gate_pre * sig
    hidden = act * up_pre
    part = jnp.sum(hidden * back, axis=1, keepdims=True)
    gate_side = back * up_pre * sig * (1.0 + gate_pre * (1.0 - sig))
    return gate_side, back * act, hidden, part


def prepare_kernel(place, rows, preacts, down_proj, sides, hidden, parts):
    slots = sides.shape[1]
    half = hidden.shape[2]
    pre = preacts[:, 0].reshape(slots, 2 * half)
    gate_side, up_side, hid, part = expert_parts(rows, pre, down_proj)
    sides[0, :, :half] = gate_side
    sides[0, :, half:] = up_side
    hidden[0] = hid
    parts[0] = jnp.broadcast_to(part, (slots, EXTRA))


def prepare(place, received, preacts, down_proj):
    columns, count, pieces, span, narrow = received.shape
    half, width = down_proj.shape
    slots = columns * span
    block = lambda m, place: (m, 0, 0)
    return pl.pallas_call(
        prepare_kernel,
        out_shape=[
            jax.ShapeDtypeStruct((count, slots, 2 * half), f32),
            jax.ShapeDtypeStruct((count, slots, half), f32),
            jax.ShapeDtypeStruct((count, slots, EXTRA), f32),
        ],
        grid_spec=pltpu.PrefetchScalarGridSpec(
            num_scalar_prefetch=1,
            grid=(count,),
            in_specs=[
                pl.BlockSpec((columns, 1, pieces, span, narrow), lambda m, place: (0, m, 0, 0, 0)),
                pl.BlockSpec((columns, 1, span, 2 * half), lambda m, place: (0, place[1 + m], 0, 0)),
                pl.BlockSpec((half, width), lambda m, place: (0, 0)),
            ],
            out_specs=[
                pl.BlockSpec((1, slots, 2 * half), block),
                pl.BlockSpec((1, slots, half), block),
                pl.BlockSpec((1, slots, EXTRA), block),
            ],
        ),
        compiler_params=params(),
        name="prepare",
    )(place, received, preacts, down_proj)


def turn_kernel(count, place, received, preacts, down_proj, gate_up, *refs):
    others, hidden, out = refs[:-2], refs[-2], refs[-1]
    half, width = down_proj.shape
    columns, _, pieces, span, _ = received.shape
    slots = columns * span
    scales = received[:, 0, pieces - 1].astype(f32).reshape(slots, EXTRA)
    gate_side, up_side, hid, part = expert_parts(received, preacts[:, 0].reshape(slots, 2 * half), down_proj)
    hidden[0] = hid
    scale = scales[:, count - 1 : count]
    both = jnp.concatenate([scale * gate_side, scale * up_side], axis=1).astype(bf16)
    for k, tile in enumerate(tiles(width)):
        grad = lax.dot_general(both, gate_up[tile, :], NT, preferred_element_type=f32)
        write_tile(out, 0, k, grad.astype(bf16))
    lane = lax.broadcasted_iota(jnp.int32, (slots, EXTRA), 1)
    parts = jnp.where(lane == count - 1, part, 0.0)
    k = 0
    for group in others:
        for m in range(group.shape[0]):
            parts = jnp.where(lane == k, group[m], parts)
            k += 1
    out[:, 0, pieces - 1] = parts.astype(bf16).reshape(columns, span, EXTRA)


def turn(place, received, preacts, down_proj, gate_up, parts):
    columns, _, pieces, span, narrow = received.shape
    half, width = down_proj.shape
    slots = columns * span
    count = 1 + sum(p.shape[0] for p in parts)
    return pl.pallas_call(
        functools.partial(turn_kernel, count),
        out_shape=[
            jax.ShapeDtypeStruct((1, slots, half), f32),
            jax.ShapeDtypeStruct((columns, 1, pieces, span, narrow), bf16),
        ],
        grid_spec=pltpu.PrefetchScalarGridSpec(
            num_scalar_prefetch=1,
            grid=(1,),
            in_specs=[
                VMEM,
                pl.BlockSpec((columns, 1, span, 2 * half), lambda m, place: (0, place[1], 0, 0)),
                VMEM,
                VMEM,
            ]
            + [VMEM] * len(parts),
            out_specs=[VMEM, VMEM],
        ),
        compiler_params=params(),
        name="turn",
    )(place, received, preacts, down_proj, gate_up, *parts)


def grad_kernel(first, sides, last, gate_up, *rest):
    out = rest[-1]
    width = gate_up.shape[0]
    columns, _, _, span, _ = out.shape
    slots = columns * span
    scales = last[:, 0, 0].reshape(slots, EXTRA).astype(f32)
    lane = lax.broadcasted_iota(jnp.int32, (slots, EXTRA), 1)
    index = first + pl.program_id(0)
    scale = jnp.sum(jnp.where(lane == index, scales, 0.0), axis=1, keepdims=True)
    both = (scale * sides[0]).astype(bf16)
    for k, tile in enumerate(tiles(width)):
        grad = lax.dot_general(both, gate_up[tile, :], NT, preferred_element_type=f32)
        write_tile(out, 0, k, grad.astype(bf16))


def slice_grad(first, offset, count, sides, last, gate_up):
    _, slots, full = sides.shape
    columns, _, _, span, _ = last.shape
    width = gate_up.shape[0]
    pieces = width // TILE
    return pl.pallas_call(
        functools.partial(grad_kernel, first),
        out_shape=jax.ShapeDtypeStruct((columns, count, pieces, span, TILE), bf16),
        grid=(count,),
        in_specs=[
            pl.BlockSpec((1, slots, full), lambda m: (offset + m, 0, 0)),
            pl.BlockSpec((columns, 1, 1, span, EXTRA), lambda m: (0, 0, width // EXTRA, 0, 0)),
            pl.BlockSpec((width, full), lambda m: (0, 0)),
        ],
        out_specs=pl.BlockSpec((columns, 1, pieces, span, TILE), lambda m: (0, m, 0, 0, 0)),
        compiler_params=params(),
        name="slice_grad",
    )(sides, last, gate_up)


def down_kernel(groups, last, *refs):
    rows, hidden, out, scaled = refs[:groups], refs[groups : 2 * groups], refs[-2], refs[-1]
    slots = hidden[0].shape[1]

    @pl.when(pl.program_id(0) == 0)
    def _():
        scales = last[:, 0, 0].reshape(slots, EXTRA).astype(f32)
        k = 0
        for group in hidden:
            for m in range(group.shape[0]):
                scaled[k * slots : (k + 1) * slots] = (scales[:, k : k + 1] * group[m]).astype(bf16)
                k += 1

    total = jnp.zeros(out.shape, f32)
    k = 0
    for group in rows:
        for m in range(group.shape[1]):
            table = read_tile(group, m, 0)
            part = scaled[k * slots : (k + 1) * slots]
            total += lax.dot_general(part, table, TN, preferred_element_type=f32)
            k += 1
    out[...] = total.astype(bf16)


def down_grads(received, hidden, width):
    last = received[-1]
    columns, _, _, span, _ = last.shape
    count = sum(h.shape[0] for h in hidden)
    slots, half = hidden[0].shape[1:]
    return pl.pallas_call(
        functools.partial(down_kernel, len(received)),
        out_shape=jax.ShapeDtypeStruct((half, width), bf16),
        grid=(width // TILE,),
        in_specs=[pl.BlockSpec((columns, 1, 1, span, EXTRA), lambda i: (0, 0, width // EXTRA, 0, 0))]
        + [
            pl.BlockSpec((columns, g.shape[1], TILE // g.shape[4], span, g.shape[4]), lambda i: (0, 0, i, 0, 0))
            for g in received
        ]
        + [pl.BlockSpec(h.shape, lambda i: (0, 0, 0)) for h in hidden],
        out_specs=pl.BlockSpec((half, TILE), lambda i: (0, i)),
        scratch_shapes=[pltpu.VMEM((count * slots, half), bf16)],
        compiler_params=params(),
        name="down_grads",
    )(last, *received, *hidden)


def fold_kernel(capacity, first, count, coming, split, place, parts, *refs):
    returned = refs[0]
    metas = refs[1 : 1 + count]
    incoming = refs[1 + count : 1 + count + coming]
    outs = refs[-3 * count :] if split else refs[-count:]
    columns, _, pieces, span, narrow = returned.shape
    table = parts[:, 0, 0].astype(f32)
    for m in range(count):
        meta = metas[m][:, :].astype(f32)
        picks = [meta[0:1, i * LANES : (i + 1) * LANES] for i in range(4)]
        hits, ids = slot_hits(picks, place[0], columns, capacity)
        ones = flat(hits)
        added = incoming[m::count] if coming >= count else incoming[m : m + 1]
        sums = [other for other in added if other.shape[0] > META]
        for n, tile in enumerate(tiles(pieces * narrow // TILE * TILE)):
            total = lax.dot_general(ones, read_tile(returned, m, n), TN, preferred_element_type=f32)
            for other in sums:
                total = total + other[:LANES, tile].astype(f32)
            total = total.astype(bf16)
            if split:
                outs[3 * m][:, tile] = total[:HALF]
                outs[3 * m + 1][:, tile] = total[HALF:]
            else:
                outs[m][:LANES, tile] = total
        values = hits * table[:, :, first + m : first + m + 1]
        for k in range(2):
            named = jnp.where(picks[k] == ids, 1.0, 0.0)[:, None, :]
            line = jnp.sum(jnp.sum(values * named, axis=1), axis=0, keepdims=True)
            lanes = slice(k * LANES, (k + 1) * LANES)
            for other in added:
                low = LANES if other.shape[0] > META else 0
                line = line + other[low : low + META, lanes].astype(f32)[0:1]
            line = jnp.broadcast_to(line, (META, LANES)).astype(bf16)
            if split:
                outs[3 * m + 2][:, lanes] = line
            else:
                outs[m][LANES : LANES + META, lanes] = line


def fold(place, first, parts, returned, arrivals, incoming, capacity, split, earlier=()):
    columns, count, _, span, _ = returned.shape
    width = arrivals[0].shape[1]
    only_tags = pl.BlockSpec((META, 4 * LANES), lambda i: (LANES // META, 0))
    if split:
        halves = [jax.ShapeDtypeStruct((HALF, width), bf16)] * 2
        shapes = (halves + [jax.ShapeDtypeStruct((META, 2 * LANES), bf16)]) * count
    else:
        shapes = [jax.ShapeDtypeStruct((LANES + META, width), bf16)] * count
    return pl.pallas_call(
        functools.partial(fold_kernel, capacity, first, count, len(incoming), split),
        out_shape=shapes,
        grid=(1,),
        in_specs=[SMEM, pl.BlockSpec((columns, 1, 1, span, EXTRA), lambda i: (0, 0, width // EXTRA, 0, 0)), VMEM]
        + [only_tags] * count
        + [VMEM] * len(incoming)
        + [ANY] * len(earlier),
        out_specs=[VMEM] * len(shapes),
        compiler_params=params(),
        name="fold_rows",
    )(place, parts, returned, *arrivals, *incoming, *earlier)


def exchange(block):
    columns, count, pieces, span, narrow = block.shape
    merged = block.reshape(columns, count * pieces, span, narrow)
    moved = lax.all_to_all(merged, "column", split_axis=0, concat_axis=0, tiled=True)
    return moved.reshape(block.shape)


def hop(block, distance):
    return lax.ppermute(block, "depth", [(i, (i + distance) % DEPTH) for i in range(DEPTH)])


def shifted(block, distance, along=0):
    sections = lax.axis_size("section")
    route = [
        (i * DEPTH + z, (i + distance) * DEPTH + (z + along) % DEPTH)
        for i in range(sections)
        for z in range(DEPTH)
        if 0 <= i + distance < sections
    ]
    return lax.ppermute(block, ("section", "depth"), route)


def shards(grad_out, gate_probs, routes, saved_preacts, w_gate_up, w_down):
    columns = lax.axis_size("column")
    capacity = saved_preacts.shape[4]
    span = 2 * capacity
    width = grad_out.shape[3]
    tokens = grad_out.shape[2]
    level = lax.axis_index("depth")
    half = level // SHARE
    gate_up = w_gate_up[0, 0]
    down_proj = w_down[0, 0]

    def place(group):
        where = [half] + [(level + DEPTH + offset) % DEPTH for offset in group]
        return jnp.stack(where).astype(jnp.int32)

    picks = jnp.moveaxis(routes[0], 2, 0).reshape(1, 4 * tokens).astype(bf16)
    gates = jnp.moveaxis(gate_probs[0], 2, 0).reshape(1, 4 * tokens)
    line = jnp.concatenate([picks, gates], axis=1)
    own = jnp.concatenate(
        [
            grad_out[0].reshape(2 * tokens, width),
            jnp.pad(line, ((0, META - 1), (0, width - line.shape[1]))),
        ]
    )
    arrivals = {0: own}
    for group in reversed(BACK[:-1]):
        for offset in group:
            toward = 1 if offset < 0 else -1
            arrivals[offset] = hop(arrivals[offset + toward], toward)
    everyone = [arrivals[offset] for group in GROUPS for offset in group]

    preacts = jnp.concatenate([saved_preacts[0, 0, 0], saved_preacts[0, 1, 0]], axis=1)
    preacts = preacts.reshape(columns, DEPTH, span, -1)
    received, sides, hidden, parts = [], [], [], []
    for n, group in enumerate(GROUPS):
        last = group == GROUPS[-1]
        earlier = sides[n - 2 : n - 1] if n >= 2 else [preacts] * n
        sent = pack(
            place(group),
            [arrivals[offset] for offset in group],
            columns,
            capacity,
            everyone if last else (),
            earlier,
        )
        got = exchange(sent)
        received.append(got)
        if not last:
            pieces = prepare(place(group), got, preacts, down_proj)
            sides.append(pieces[0])
            hidden.append(pieces[1])
            parts.append(pieces[2])
    last = received[-1]
    final_hidden, sending = turn(place(GROUPS[-1]), last, preacts, down_proj, gate_up, parts)
    hidden.append(final_hidden)

    listed = [offset for group in GROUPS for offset in group]
    part_rows = None
    coming = []
    for n, group in enumerate(BACK):
        returned = exchange(sending)
        if part_rows is None:
            part_rows = returned
        earlier = []
        if n + 1 < len(BACK):
            following = BACK[n + 1]
            start = listed.index(following[0])
            source = [following[0] in g for g in GROUPS].index(True)
            held = list(coming)
            if n == 2:
                down_grad = down_grads(received, hidden, width)
                held.append(down_grad)
            sending = slice_grad(
                start,
                GROUPS[source].index(following[0]),
                len(following),
                sides[source],
                last,
                gate_up,
            )
            sending = ordered(sending, *held) if held else sending
            earlier = [sending]
        folded = fold(
            place(group),
            listed.index(group[0]),
            part_rows,
            returned,
            [arrivals[offset] for offset in group],
            coming,
            capacity,
            n >= len(BACK) - 2,
            earlier,
        )
        along = [-1 if offset < 0 else 1 for offset in group]
        if n < len(BACK) - 2:
            coming = [hop(block, way) for block, way in zip(folded, along)]
        elif n == len(BACK) - 2:
            coming = [hop(folded[3 * m + 2], way) for m, way in enumerate(along)]
            above = [shifted(folded[3 * m], -1, way) for m, way in enumerate(along)]
            below = [shifted(folded[3 * m + 1], 1, way) for m, way in enumerate(along)]
    above.append(shifted(folded[0], -1))
    below.append(shifted(folded[1], 1))
    from_above = sum(part.astype(f32) for part in above).astype(bf16)
    from_below = sum(part.astype(f32) for part in below).astype(bf16)
    prob_grad = jnp.moveaxis(folded[2][0].astype(f32).reshape(2, 2, tokens), 0, 2)
    return (from_above[None], from_below[None], prob_grad[None], down_grad[None, None])


def solution(mesh):
    sections, slices = mesh.devices.shape
    grid = Mesh(mesh.devices.reshape(sections, slices // DEPTH, DEPTH), ("section", "column", "depth"))
    spread = ("column", "depth")
    in_specs = (
        P("section", None, spread, None),
        P("section", None, spread, None),
        P("section", None, spread, None),
        P("section", None, spread, None, None, None),
        P("section", spread, None, None),
        P("section", spread, None, None),
    )
    out_specs = (
        P("section", spread, None),
        P("section", spread, None),
        P("section", None, spread, None),
        P("section", spread, None, None),
    )
    return jax.shard_map(shards, mesh=grid, in_specs=in_specs, out_specs=out_specs, check_vma=False)
```
